512 devices in a mesh: segment: 16 (over z_lo, x), dp: 8 (over y, core), mp: 4 (over z_hi).
Axes of the slice: x: 4, y: 4, z: 16 (z_hi: 4, z_lo: 4; z = z_hi * 4 + z_lo), core: 2. Of those that a mesh axis runs over, the one named last changes fastest.
Arguments:
- encoder_image_states: bfloat16 [8, 128, 8192], P('dp', 'segment'), may hold values from -6 to 6
- frozen_key_value: bfloat16 [16, 8192, 2, 1024], P('segment', 'dp', None, 'mp'), may hold values from -0.0625 to 0.0625
- adapter_down_weight: bfloat16 [16, 8192, 128], P('segment', 'mp'), may hold values from -0.0625 to 0.0625
- adapter_up_weight: bfloat16 [16, 2, 64, 1024], P('segment', None, None, 'mp'), may hold values from -0.75 to 0.75
- queries: bfloat16 [16, 8, 128, 8192], P('segment', 'dp', None, 'mp'), may hold values from -9 to 9
- cotangent: bfloat16 [16, 8, 128, 8192], P('segment', 'dp', None, 'mp'), may hold values from -1.5 to 1.5
- text_token_length: int32 [8], P('dp'), may hold values from 32 to 128
- image_tile_count: int32 [8], P('dp'), may hold values from 1 to 4
Outputs:
- grad_down: bfloat16 [16, 8192, 128], P('segment', 'mp')
- up_gradient: bfloat16 [16, 2, 64, 1024], P('segment', None, None, 'mp')
- grad_image: float32 [8, 128, 8192], P('dp', 'segment')
The draws below stay inside these ranges and needn't reach their ends.
All inputs are finite; a program needn't handle non-finite values.
Results may differ from the reference program's by a relative error of at most 0.017.
The reference program's roundings to bfloat16 on the way count: a program that leaves them out, or rounds other values in their place, can miss the bound.
Values may be sent and summed in bfloat16 or wider, within the bound.
No kernel may reach another device: no remote copies, remote signals or barrier semaphores. Data moves between devices by JAX's collectives and lax.ppermute only.
A program may use at most 64 MiB of HBM per device.

```python
import jax
import jax.numpy as jnp
from jax import lax

MODEL_DIM = 8192
H = 64
HD = 128
TILES = 4
ADAPTER_RANK = 64
TXT = 128
CROSS_LAYERS = 16
SAMPLE_COUNT = 8
IMAGE_TOKENS = 128
KEY_VALUE_COLS = 1024


def draw_queries(key, part):
    base_key = jax.random.fold_in(jax.random.fold_in(key, 7), 0)
    array_shape = (CROSS_LAYERS, SAMPLE_COUNT, TXT, H * HD)
    values = jnp.clip(jax.random.normal(base_key, array_shape, jnp.float32), -5.0, 5.0)
    return values.astype(jnp.bfloat16)


def touch_ends(values, stream_key, least, largest):
    spot = [jax.random.randint(jax.random.fold_in(stream_key, axis), (), 0, length) for axis, length in enumerate(values.shape)]
    longest = values.shape.index(max(values.shape))
    neighbour = spot[:longest] + [(spot[longest] + 1) % values.shape[longest]] + spot[longest + 1:]
    return values.at[tuple(spot)].set(least).at[tuple(neighbour)].set(largest)


def level_of(own_key, extent, shards, smallest, largest):
    gain = 1.0
    for dim, blocks in shards:
        heights = jax.random.uniform(jax.random.fold_in(jax.random.fold_in(own_key, 6), dim), (blocks,), jnp.float32, smallest / len(shards), largest / len(shards))
        gain = gain * jnp.repeat(jnp.exp(heights), extent[dim] // blocks).reshape((-1,) + (1,) * (len(extent) - 1 - dim))
    return gain


def scatter_about(stream_key, shape, deviation, most, pieces=(), kind=jnp.bfloat16):
    result = jax.random.normal(stream_key, shape, jnp.float32) * deviation
    if len(pieces) > 0:
        result = level_of(stream_key, shape, pieces, -0.22, 0.18) * result
    return jnp.clip(result, min=-most, max=most).astype(kind)


def setup_inputs(seed: int = 0) -> dict:
    key_list = jax.random.split(jax.random.key(seed), 9)
    encoder_image_states = scatter_about(key_list[0], (SAMPLE_COUNT, IMAGE_TOKENS, MODEL_DIM), 1.0, 6.0, ((0, 8), (1, 16)))
    frozen_key_value = scatter_about(key_list[1], (CROSS_LAYERS, MODEL_DIM, 2, KEY_VALUE_COLS), MODEL_DIM ** -0.5, 0.0625, ((0, 16), (1, 8), (3, 4)))
    adapter_down_weight = scatter_about(key_list[2], (CROSS_LAYERS, MODEL_DIM, 2 * ADAPTER_RANK), MODEL_DIM ** -0.5, 0.0625, ((0, 16), (1, 4)))
    adapter_up_weight = scatter_about(key_list[3], (CROSS_LAYERS, 2, ADAPTER_RANK, KEY_VALUE_COLS), ADAPTER_RANK ** -0.5, 0.75, ((0, 16), (3, 4)))
    queries = draw_queries(jax.random.fold_in(key_list[8], 71), 0)
    cotangent = scatter_about(key_list[5], (CROSS_LAYERS, SAMPLE_COUNT, TXT, H * HD), 0.25, 1.5, ((0, 16), (1, 8), (3, 4)))
    text_token_length = touch_ends(jax.random.randint(key_list[6], (SAMPLE_COUNT,), TXT // 4, TXT + 1), jax.random.fold_in(key_list[6], 1), TXT // 4, TXT).astype(jnp.int32)
    image_tile_count = touch_ends(jax.random.randint(key_list[7], (SAMPLE_COUNT,), 1, TILES + 1), jax.random.fold_in(key_list[7], 1), 1, TILES).astype(jnp.int32)
    return dict(encoder_image_states=encoder_image_states, frozen_key_value=frozen_key_value, adapter_down_weight=adapter_down_weight, adapter_up_weight=adapter_up_weight, queries=queries, cotangent=cotangent, text_token_length=text_token_length, image_tile_count=image_tile_count)


adapter_scale = 2.0


def layer_terms(image_flat, key_mask, row_mask, frozen, down_proj, up_proj, query_in, cot_in):
    lowrank_state = up_proj.shape[1]
    model_width = frozen.shape[0]
    key_value_columns = frozen.shape[2]
    samples = query_in.shape[0]
    text_rows = query_in.shape[1]
    image_rows = image_flat.shape[0] // samples
    kv_heads = key_value_columns // HD
    group_size = query_in.shape[2] // (HD * kv_heads)
    lowrank_projection = jnp.dot(image_flat, down_proj, preferred_element_type=jnp.float32).astype(jnp.bfloat16)
    adapted_weight = jnp.concatenate([
        jnp.dot(lowrank_projection[:, :lowrank_state], up_proj[0], preferred_element_type=jnp.float32),
        jnp.dot(lowrank_projection[:, lowrank_state:], up_proj[1], preferred_element_type=jnp.float32)], axis=1)
    weight_flat = frozen.reshape(model_width, 2 * key_value_columns)
    frozen_output = jnp.dot(image_flat, weight_flat, preferred_element_type=jnp.float32)
    key_value_pair = (frozen_output + adapter_scale * adapted_weight).astype(jnp.bfloat16)
    key_rows = key_value_pair[:, :key_value_columns].reshape(samples, image_rows, kv_heads, HD).astype(jnp.float32)
    value_rows = key_value_pair[:, key_value_columns:].reshape(samples, image_rows, kv_heads, HD).astype(jnp.float32)
    query_rows = query_in.reshape(samples, text_rows, kv_heads, group_size, HD).astype(jnp.float32)
    cot_rows = cot_in.reshape(samples, text_rows, kv_heads, group_size, HD).astype(jnp.float32)
    scores = jnp.einsum("btgrd,bjgd->bgrtj", query_rows, key_rows) * (HD ** -0.5)
    masked = jnp.where(key_mask[:, None, None, None, :], scores, -1e30)
    row_top = jnp.max(masked, axis=-1, keepdims=True)
    shifted = jnp.exp(masked - row_top)
    attention = shifted / jnp.sum(shifted, axis=-1, keepdims=True)
    row_gate = row_mask[:, None, None, :, None]
    kept = attention.astype(jnp.bfloat16) * row_gate.astype(jnp.bfloat16)
    dweights = jnp.einsum("btgrd,bjgd->bgrtj", cot_rows, value_rows)
    row_delta = jnp.sum(attention * dweights, axis=-1, keepdims=True)
    dscore = (attention * (dweights - row_delta) * row_gate * (HD ** -0.5)).astype(jnp.bfloat16)
    key_grad = jnp.einsum("bgrtj,btgrd->bjgd", dscore.astype(jnp.float32), query_rows)
    value_grad = jnp.einsum("bgrtj,btgrd->bjgd", kept.astype(jnp.float32), cot_rows)
    flat_rows = samples * image_rows
    kv_grad = jnp.concatenate([key_grad.reshape(flat_rows, key_value_columns), value_grad.reshape(flat_rows, key_value_columns)], axis=1).astype(jnp.bfloat16)
    backward_lowrank = (adapter_scale * jnp.concatenate([
        jnp.dot(kv_grad[:, :key_value_columns], up_proj[0].T, preferred_element_type=jnp.float32),
        jnp.dot(kv_grad[:, key_value_columns:], up_proj[1].T, preferred_element_type=jnp.float32)], axis=1)).astype(jnp.bfloat16)
    up_gradient = adapter_scale * jnp.stack([
        jnp.dot(lowrank_projection[:, :lowrank_state].T, kv_grad[:, :key_value_columns], preferred_element_type=jnp.float32),
        jnp.dot(lowrank_projection[:, lowrank_state:].T, kv_grad[:, key_value_columns:], preferred_element_type=jnp.float32)])
    grad_down = jnp.dot(image_flat.T, backward_lowrank, preferred_element_type=jnp.float32)
    grad_img = jnp.dot(kv_grad, weight_flat.T, preferred_element_type=jnp.float32) + jnp.dot(backward_lowrank, down_proj.T, preferred_element_type=jnp.float32)
    return grad_down, up_gradient, grad_img


def reference(encoder_image_states, frozen_key_value, adapter_down_weight, adapter_up_weight, queries, cotangent, text_token_length, image_tile_count):
    image_flat = encoder_image_states.reshape(SAMPLE_COUNT * IMAGE_TOKENS, MODEL_DIM)
    key_mask = jnp.arange(IMAGE_TOKENS, dtype=jnp.int32)[None, :] < (image_tile_count[:, None] * (IMAGE_TOKENS // TILES)).astype(jnp.int32)
    row_mask = (jnp.arange(TXT, dtype=jnp.int32)[None, :] < text_token_length[:, None].astype(jnp.int32)).astype(jnp.float32)

    def accumulate_terms(running_total, layer_in):
        frozen, down_proj, up_proj, query_in, cot_in = layer_in
        grad_down, up_gradient, grad_img = layer_terms(image_flat, key_mask, row_mask, frozen, down_proj, up_proj, query_in, cot_in)
        return running_total + grad_img, (grad_down.astype(jnp.bfloat16), up_gradient.astype(jnp.bfloat16))

    running_total, stacked_layers = lax.scan(accumulate_terms, jnp.zeros((SAMPLE_COUNT * IMAGE_TOKENS, MODEL_DIM), jnp.float32), (frozen_key_value, adapter_down_weight, adapter_up_weight, queries, cotangent))
    return stacked_layers[0], stacked_layers[1], running_total.reshape(SAMPLE_COUNT, IMAGE_TOKENS, MODEL_DIM)
```

```python
import jax
import jax.numpy as jnp
from jax import lax
from jax.sharding import PartitionSpec as P

HD = 128
TILES = 4
SIDE = 4

adapter_scale = 2.0
contract_rows = (((0,), (0,)), ((), ()))
contracted_columns = (((1,), (1,)), ((), ()))
f32 = jnp.float32
bf16 = jnp.bfloat16
AXES = ("segment", "dp", "mp")


def make_body(mesh):
    segments, parts, heads = (mesh.shape[a] for a in AXES)
    runs = segments // SIDE
    ring = runs * heads

    def shift(v, dx, dz, opposite=False):
        pairs = []
        for s in range(segments):
            for d in range(parts):
                for m in range(heads):
                    z_lo, x = divmod(s, SIDE)
                    sign = -1 if (opposite and d % 2) else 1
                    x2 = (x + sign * dx) % SIDE
                    m2, z2 = divmod((m * runs + z_lo + sign * dz) % ring, runs)
                    pairs.append(((s * parts + d) * heads + m, ((z2 * SIDE + x2) * parts + d) * heads + m2))
        return lax.ppermute(v, AXES, pairs)

    def sum_over_mp(v):
        return jnp.sum(lax.all_gather(v, "mp", axis=0), axis=0)

    def body(
        encoder_image_states,
        frozen_key_value,
        adapter_down_weight,
        adapter_up_weight,
        queries,
        cotangent,
        text_token_length,
        image_tile_count,
    ):
        own = encoder_image_states[0]
        tokens, model_width = own.shape
        parallel_index = lax.axis_index("mp")
        segment_index = lax.axis_index("segment")
        lowrank = adapter_up_weight.shape[2]
        columns = adapter_up_weight.shape[3]
        up_key, up_value = adapter_up_weight[0, 0], adapter_up_weight[0, 1]
        down = adapter_down_weight[0]
        fourth = down.shape[0]

        local_weight = frozen_key_value[0].reshape(-1, 2 * columns)
        weight = lax.all_gather(local_weight, "dp", axis=0, tiled=True)

        line = jnp.concatenate([own, shift(own, 0, -1), shift(own, 0, 2, True), shift(own, 0, 1)], axis=0)
        image = jnp.concatenate([line, shift(line, -1, 0), shift(line, 2, 0, True), shift(line, 1, 0)], axis=0)
        rows = image.shape[0]
        offset = jnp.arange(rows, dtype=jnp.int32)
        x_off, z_off, tok = offset // (runs * tokens), (offset // tokens) % runs, offset % tokens
        position = (
            ((segment_index // SIDE + z_off) % runs) * SIDE + (segment_index % SIDE + x_off) % SIDE
        ) * tokens + tok

        image_fourth = lax.dynamic_slice_in_dim(image, parallel_index * fourth, fourth, 1)
        low = sum_over_mp(jnp.dot(image_fourth, down, preferred_element_type=f32)).astype(bf16)
        adapted = jnp.concatenate(
            [
                jnp.dot(low[:, :lowrank], up_key, preferred_element_type=f32),
                jnp.dot(low[:, lowrank:], up_value, preferred_element_type=f32),
            ],
            axis=1,
        )
        key_value = (jnp.dot(image, weight, preferred_element_type=f32) + adapter_scale * adapted).astype(bf16)

        local_kv = columns // HD
        text_rows = queries.shape[2]
        group = queries.shape[3] // HD // local_kv
        query_rows = queries[0, 0].reshape(text_rows, local_kv, group, HD)
        cot_rows = cotangent[0, 0].reshape(text_rows, local_kv, group, HD)
        key_rows = key_value[:, :columns].reshape(rows, local_kv, HD)
        value_rows = key_value[:, columns:].reshape(rows, local_kv, HD)
        key_mask = position < image_tile_count[0] * (rows // TILES)
        row_mask = (jnp.arange(text_rows, dtype=jnp.int32) < text_token_length[0]).astype(f32)
        scores = jnp.einsum("tgrd,jgd->grtj", query_rows, key_rows, preferred_element_type=f32) * HD ** (-0.5)
        masked = jnp.where(key_mask[None, None, None, :], scores, -1e30)
        row_top = jnp.max(masked, axis=-1, keepdims=True)
        shifted = jnp.exp(masked - row_top)
        attention = shifted / jnp.sum(shifted, axis=-1, keepdims=True)
        row_gate = row_mask[None, None, :, None]
        kept = attention.astype(bf16) * row_gate.astype(bf16)
        dweights = jnp.einsum("tgrd,jgd->grtj", cot_rows, value_rows, preferred_element_type=f32)
        row_delta = jnp.sum(attention * dweights, axis=-1, keepdims=True)
        dscore = (attention * (dweights - row_delta) * row_gate * HD ** (-0.5)).astype(bf16)
        key_grad = jnp.einsum("grtj,tgrd->jgd", dscore, query_rows, preferred_element_type=f32)
        value_grad = jnp.einsum("grtj,tgrd->jgd", kept, cot_rows, preferred_element_type=f32)
        kv_grad = jnp.concatenate(
            [key_grad.reshape(rows, columns), value_grad.reshape(rows, columns)], axis=1
        ).astype(bf16)

        block = runs * tokens
        mine = lax.dot_general(kv_grad[:block], weight, contracted_columns, preferred_element_type=f32)
        away = lax.dot_general(kv_grad[block:], weight, contracted_columns, preferred_element_type=f32).astype(bf16)

        def over_x(stay, leave):
            a = shift(leave[:block], 1, 0)
            b = shift(leave[block : 2 * block], 2, 0, True)
            c = shift(leave[2 * block :], -1, 0)
            return stay + a.astype(f32) + b.astype(f32) + c.astype(f32)

        image_grad = over_x(mine, away)

        back = sum_over_mp(
            adapter_scale
            * jnp.concatenate(
                [
                    lax.dot_general(kv_grad[:, :columns], up_key, contracted_columns, preferred_element_type=f32),
                    lax.dot_general(kv_grad[:, columns:], up_value, contracted_columns, preferred_element_type=f32),
                ],
                axis=1,
            )
        ).astype(bf16)
        adapter_grad = lax.dot_general(back, down, contracted_columns, preferred_element_type=f32)
        adapter_grad = over_x(adapter_grad[:block], adapter_grad[block:].astype(bf16))

        down_grad = lax.dot_general(image_fourth, back, contract_rows, preferred_element_type=f32)
        up_grad = adapter_scale * jnp.stack(
            [
                lax.dot_general(low[:, :lowrank], kv_grad[:, :columns], contract_rows, preferred_element_type=f32),
                lax.dot_general(low[:, lowrank:], kv_grad[:, columns:], contract_rows, preferred_element_type=f32),
            ]
        )
        both = jnp.concatenate([down_grad, up_grad.reshape(-1, down_grad.shape[1])], axis=0)
        both = lax.psum_scatter(both, "dp", scatter_dimension=0, tiled=True).astype(bf16)
        both = lax.all_gather(both, "dp", axis=0, tiled=True)
        down_out = both[:fourth]
        up_out = both[fourth:].reshape(up_grad.shape)

        here = lax.dynamic_slice_in_dim(image_grad, parallel_index * fourth, fourth, 1)
        image_grad = lax.dynamic_update_slice_in_dim(
            image_grad, here + adapter_grad, parallel_index * fourth, 1
        )
        send = image_grad[tokens:].astype(bf16)
        image_grad = (
            image_grad[:tokens]
            + shift(send[:tokens], 0, 1).astype(f32)
            + shift(send[tokens : 2 * tokens], 0, 2, True).astype(f32)
            + shift(send[2 * tokens :], 0, -1).astype(f32)
        )
        quarters = image_grad.reshape(tokens, heads, fourth).transpose(1, 0, 2)
        quarter = jnp.sum(lax.all_to_all(quarters, "mp", 0, 0), axis=0)
        result = lax.all_gather(quarter, "mp", axis=1, tiled=True)
        return (down_out[None], up_out[None], result[None])

    return body


def solution(mesh):
    in_specs = (
        P("dp", "segment", None),
        P("segment", "dp", None, "mp"),
        P("segment", "mp", None),
        P("segment", None, None, "mp"),
        P("segment", "dp", None, "mp"),
        P("segment", "dp", None, "mp"),
        P("dp"),
        P("dp"),
    )
    out_specs = (P("segment", "mp", None), P("segment", None, None, "mp"), P("dp", "segment", None))
    return jax.shard_map(make_body(mesh), mesh=mesh, in_specs=in_specs, out_specs=out_specs, check_vma=False)
```

```python
import jax
import jax.numpy as jnp
from jax import lax
from jax.sharding import PartitionSpec as P


HD = 128
TILES = 4
SIDE = 4
CORES = 2

adapter_scale = 2.0
contract_rows = (((0,), (0,)), ((), ()))
contracted_columns = (((1,), (1,)), ((), ()))
f32 = jnp.float32
bf16 = jnp.bfloat16
AXES = ("segment", "dp", "mp")


def make_body(mesh):
    segments, parts, heads = (mesh.shape[a] for a in AXES)
    runs = segments // SIDE
    ring = runs * heads
    lines = parts // CORES

    def shift(v, dx=0, dy=0, dz=0, swap=0, opposite=False):
        pairs = []
        for s in range(segments):
            for d in range(parts):
                for m in range(heads):
                    z_lo, x = divmod(s, SIDE)
                    y, core = divmod(d, CORES)
                    sign = -1 if (opposite and core) else 1
                    x2 = (x + sign * dx) % SIDE
                    d2 = (y + sign * dy) % lines * CORES + (core + swap) % CORES
                    m2, z2 = divmod((m * runs + z_lo + sign * dz) % ring, runs)
                    pairs.append(((s * parts + d) * heads + m, ((z2 * SIDE + x2) * parts + d2) * heads + m2))
        return lax.ppermute(v, AXES, pairs)

    def sum_over_mp(v, out):
        far = shift(v, dz=2 * runs, opposite=True)
        near = shift(v, dz=runs)
        prior = shift(v, dz=-runs)
        return ((v.astype(f32) + far.astype(f32)) + (near.astype(f32) + prior.astype(f32))).astype(out)

    def body(
        encoder_image_states,
        frozen_key_value,
        adapter_down_weight,
        adapter_up_weight,
        queries,
        cotangent,
        text_token_length,
        image_tile_count,
    ):
        tokens, model_width = encoder_image_states.shape[1:]
        parallel_index = lax.axis_index("mp")
        segment_index = lax.axis_index("segment")
        part_index = lax.axis_index("dp")
        y_index, core_index = part_index // CORES, part_index % CORES
        second_core = core_index == 1
        lowrank = adapter_up_weight.shape[2]
        columns = adapter_up_weight.shape[3]
        up_key, up_value = adapter_up_weight[0, 0], adapter_up_weight[0, 1]
        down = adapter_down_weight[0]
        fourth = down.shape[0]
        eighth = fourth // CORES

        def swap_halves(v, axis):
            a, b = jnp.split(v, CORES, axis=axis)
            return jnp.where(second_core, jnp.concatenate([b, a], axis=axis), v)

        def swap_chunks(v):
            w = v.reshape(v.shape[0], lines, CORES, eighth)
            return jnp.where(second_core, w[:, :, ::-1], w).reshape(v.shape)

        def roll_columns(v, by):
            return lax.dynamic_slice_in_dim(jnp.concatenate([v, v], axis=1), by * fourth, model_width, 1)

        own = swap_chunks(roll_columns(encoder_image_states[0], y_index))
        down = swap_halves(down, 0)
        chunk_pair = (parallel_index - y_index) % lines

        line = jnp.concatenate([own, shift(own, dz=-1), shift(own, dz=2, opposite=True), shift(own, dz=1)], axis=0)
        image = jnp.concatenate([line, shift(line, dx=-1), shift(line, dx=2, opposite=True), shift(line, dx=1)], axis=0)
        rows = image.shape[0]
        offset = jnp.arange(rows, dtype=jnp.int32)
        x_off, z_off, tok = offset // (runs * tokens), (offset // tokens) % runs, offset % tokens
        position = (
            ((segment_index // SIDE + z_off) % runs) * SIDE + (segment_index % SIDE + x_off) % SIDE
        ) * tokens + tok

        local_weight = frozen_key_value[0].reshape(-1, CORES * columns)
        half = local_weight.shape[0] // 2
        following = shift(local_weight, dy=-1)
        preceding = shift(local_weight, dy=1)
        first_half, second_half = following[:half], preceding[half:]
        across_a = shift(first_half, dy=-1)
        across_b = shift(second_half, dy=1)
        weight = jnp.concatenate(
            [
                local_weight,
                shift(local_weight, swap=1),
                following,
                shift(following, swap=1),
                across_a,
                across_b,
                shift(across_a, swap=1),
                shift(across_b, swap=1),
                preceding,
                shift(preceding, swap=1),
            ],
            axis=0,
        )

        image_fourth = lax.dynamic_slice_in_dim(image, chunk_pair * fourth, fourth, 1)
        low = jnp.dot(image_fourth, down, preferred_element_type=f32)
        low = sum_over_mp(low, bf16)
        adapted = jnp.concatenate(
            [
                jnp.dot(low[:, :lowrank], up_key, preferred_element_type=f32),
                jnp.dot(low[:, lowrank:], up_value, preferred_element_type=f32),
            ],
            axis=1,
        )
        key_value = (jnp.dot(image, weight, preferred_element_type=f32) + adapter_scale * adapted).astype(bf16)

        local_kv = columns // HD
        text_rows = queries.shape[2]
        group = queries.shape[3] // HD // local_kv
        query_rows = queries[0, 0].reshape(text_rows, local_kv, group, HD)
        cot_rows = cotangent[0, 0].reshape(text_rows, local_kv, group, HD)
        key_rows = key_value[:, :columns].reshape(rows, local_kv, HD)
        value_rows = key_value[:, columns:].reshape(rows, local_kv, HD)
        key_mask = position < image_tile_count[0] * (rows // TILES)
        row_mask = (jnp.arange(text_rows, dtype=jnp.int32) < text_token_length[0]).astype(f32)
        scores = jnp.einsum("tgrd,jgd->grtj", query_rows, key_rows, preferred_element_type=f32) * HD ** (-0.5)
        masked = jnp.where(key_mask[None, None, None, :], scores, -1e30)
        row_top = jnp.max(masked, axis=-1, keepdims=True)
        shifted = jnp.exp(masked - row_top)
        attention = shifted / jnp.sum(shifted, axis=-1, keepdims=True)
        row_gate = row_mask[None, None, :, None]
        kept = attention.astype(bf16) * row_gate.astype(bf16)
        dweights = jnp.einsum("tgrd,jgd->grtj", cot_rows, value_rows, preferred_element_type=f32)
        row_delta = jnp.sum(attention * dweights, axis=-1, keepdims=True)
        dscore = (attention * (dweights - row_delta) * row_gate * HD ** (-0.5)).astype(bf16)
        key_grad = jnp.einsum("grtj,tgrd->jgd", dscore, query_rows, preferred_element_type=f32)
        value_grad = jnp.einsum("grtj,tgrd->jgd", kept, cot_rows, preferred_element_type=f32)
        kv_grad = jnp.concatenate(
            [key_grad.reshape(rows, columns), value_grad.reshape(rows, columns)], axis=1
        ).astype(bf16)

        block = runs * tokens

        def over_x(v):
            v = v.astype(bf16)
            a = shift(v[block : 2 * block], dx=1)
            b = shift(v[2 * block : 3 * block], dx=2, opposite=True)
            c = shift(v[3 * block :], dx=-1)
            return v[:block].astype(f32) + a.astype(f32) + b.astype(f32) + c.astype(f32)

        image_grad = over_x(lax.dot_general(kv_grad, weight, contracted_columns, preferred_element_type=f32))

        back = adapter_scale * jnp.concatenate(
            [
                lax.dot_general(kv_grad[:, :columns], up_key, contracted_columns, preferred_element_type=f32),
                lax.dot_general(kv_grad[:, columns:], up_value, contracted_columns, preferred_element_type=f32),
            ],
            axis=1,
        )
        back = lax.all_gather(back, "mp", axis=0)
        back = jnp.sum(back, axis=0).astype(bf16)
        adapter_grad = over_x(lax.dot_general(back, down, contracted_columns, preferred_element_type=f32))

        down_grad = lax.dot_general(image_fourth, back, contract_rows, preferred_element_type=f32)
        up_grad = adapter_scale * jnp.stack(
            [
                lax.dot_general(low[:, :lowrank], kv_grad[:, :columns], contract_rows, preferred_element_type=f32),
                lax.dot_general(low[:, lowrank:], kv_grad[:, columns:], contract_rows, preferred_element_type=f32),
            ]
        )
        both = jnp.concatenate(
            [swap_halves(down_grad, 0), up_grad.reshape(-1, down_grad.shape[1])], axis=0
        ).reshape(lines, CORES, -1, down_grad.shape[1])
        kept_core = lax.dynamic_index_in_dim(both, core_index, 1, keepdims=False)
        sent_core = lax.dynamic_index_in_dim(both, 1 - core_index, 1, keepdims=False)
        pair = kept_core + shift(sent_core, swap=1)

        def for_line(r):
            return lax.dynamic_index_in_dim(pair, (y_index + r) % lines, 0, keepdims=False)

        both = (
            for_line(0)
            + shift(for_line(1), dy=1)
            + shift(for_line(2), dy=2, opposite=True)
            + shift(for_line(3), dy=-1)
        ).astype(bf16)

        here = lax.dynamic_slice_in_dim(image_grad, chunk_pair * fourth, fourth, 1)
        image_grad = lax.dynamic_update_slice_in_dim(image_grad, here + adapter_grad, chunk_pair * fourth, 1)
        send = image_grad[tokens:].astype(bf16)
        image_grad = (
            image_grad[:tokens]
            + shift(send[:tokens], dz=1).astype(f32)
            + shift(send[tokens : 2 * tokens], dz=2, opposite=True).astype(f32)
            + shift(send[2 * tokens :], dz=-1).astype(f32)
        )
        image_grad = sum_over_mp(image_grad.astype(bf16), f32)
        both = lax.all_gather(both, "dp", axis=0, tiled=True)
        down_out = both[:fourth]
        up_out = both[fourth:].reshape(up_grad.shape)
        result = roll_columns(swap_chunks(image_grad), (lines - y_index) % lines)
        return (down_out[None], up_out[None], result[None])

    return body


def solution(mesh):
    in_specs = (
        P("dp", "segment", None),
        P("segment", "dp", None, "mp"),
        P("segment", "mp", None),
        P("segment", None, None, "mp"),
        P("segment", "dp", None, "mp"),
        P("segment", "dp", None, "mp"),
        P("dp"),
        P("dp"),
    )
    out_specs = (P("segment", "mp", None), P("segment", None, None, "mp"), P("dp", "segment", None))
    body = make_body(mesh)

    return jax.shard_map(body, mesh=mesh, in_specs=in_specs, out_specs=out_specs, check_vma=False)
```

```python
import jax
import jax.numpy as jnp
from jax import lax
from jax.experimental import pallas as pl
from jax.sharding import PartitionSpec as P


HD = 128
TILES = 4
SIDE = 4
CORES = 2

adapter_scale = 2.0
contract_rows = (((0,), (0,)), ((), ()))
contracted_columns = (((1,), (1,)), ((), ()))
f32 = jnp.float32
bf16 = jnp.bfloat16
AXES = ("segment", "dp", "mp")


def image_grad_kernel(kv_ref, back_ref, weight_ref, down_ref, own_ref, *away_refs):
    down = down_ref[...].reshape(weight_ref.shape[0], back_ref.shape[1])
    total = lax.dot_general(kv_ref[...], weight_ref[...], contracted_columns, preferred_element_type=f32)
    total += lax.dot_general(back_ref[...], down, contracted_columns, preferred_element_type=f32)
    block = own_ref.shape[0]
    own_ref[...] = total[:block]
    for i, ref in enumerate(away_refs):
        ref[...] = total[(i + 1) * block : (i + 2) * block].astype(bf16)


def image_grad_blocks(kv_grad, back, weight, down):
    rows, columns = kv_grad.shape
    width = weight.shape[0]
    parts, _, slice_rows, rank = down.shape
    share = parts // CORES
    step = share * slice_rows
    block = rows // SIDE
    out_spec = pl.BlockSpec((block, step), lambda j: (0, j))
    return pl.pallas_call(
        image_grad_kernel,
        grid=(width // step,),
        in_specs=[
            pl.BlockSpec((rows, columns), lambda j: (0, 0)),
            pl.BlockSpec((rows, rank), lambda j: (0, 0)),
            pl.BlockSpec((step, columns), lambda j: (j, 0)),
            pl.BlockSpec((share, 1, slice_rows, rank), lambda j: (j % CORES, j // CORES, 0, 0)),
        ],
        out_specs=[out_spec] * SIDE,
        out_shape=[jax.ShapeDtypeStruct((block, width), f32)]
        + [jax.ShapeDtypeStruct((block, width), bf16)] * (SIDE - 1),
        name="image_grad",
    )(kv_grad, back, weight, down)


def make_body(mesh):
    segments, parts, heads = (mesh.shape[a] for a in AXES)
    runs = segments // SIDE
    ring = runs * heads

    def shift(v, dx=0, dz=0, opposite=False):
        pairs = []
        for s in range(segments):
            for d in range(parts):
                for m in range(heads):
                    z_lo, x = divmod(s, SIDE)
                    sign = -1 if (opposite and d % CORES) else 1
                    x2 = (x + sign * dx) % SIDE
                    m2, z2 = divmod((m * runs + z_lo + sign * dz) % ring, runs)
                    pairs.append(((s * parts + d) * heads + m, ((z2 * SIDE + x2) * parts + d) * heads + m2))
        return lax.ppermute(v, AXES, pairs)

    def sum_over_mp(v, out):
        far = shift(v, dz=2 * runs, opposite=True)
        near = shift(v, dz=runs)
        prior = shift(v, dz=-runs)
        return ((v.astype(f32) + far.astype(f32)) + (near.astype(f32) + prior.astype(f32))).astype(out)

    def body(
        encoder_image_states,
        frozen_key_value,
        adapter_down_weight,
        adapter_up_weight,
        queries,
        cotangent,
        text_token_length,
        image_tile_count,
    ):
        own = encoder_image_states[0]
        tokens, _ = own.shape
        parallel_index = lax.axis_index("mp")
        segment_index = lax.axis_index("segment")
        lowrank = adapter_up_weight.shape[2]
        columns = adapter_up_weight.shape[3]
        up_key, up_value = adapter_up_weight[0, 0], adapter_up_weight[0, 1]
        down = adapter_down_weight[0]
        fourth = down.shape[0]

        line = jnp.concatenate([own, shift(own, dz=-1), shift(own, dz=2, opposite=True), shift(own, dz=1)], axis=0)
        image = jnp.concatenate([line, shift(line, dx=-1), shift(line, dx=2, opposite=True), shift(line, dx=1)], axis=0)
        rows = image.shape[0]
        offset = jnp.arange(rows, dtype=jnp.int32)
        x_off, z_off, tok = offset // (runs * tokens), (offset // tokens) % runs, offset % tokens
        position = (
            ((segment_index // SIDE + z_off) % runs) * SIDE + (segment_index % SIDE + x_off) % SIDE
        ) * tokens + tok

        local_weight = frozen_key_value[0].reshape(-1, CORES * columns)
        weight = lax.all_gather(local_weight, "dp", axis=0, tiled=True)
        slice_rows = fourth // parts
        down_slices = lax.all_gather(
            lax.dynamic_slice_in_dim(down, lax.axis_index("dp") * slice_rows, slice_rows, 0),
            "mp",
            axis=0,
            tiled=True,
        )
        all_down = lax.all_gather(down_slices, "dp", axis=0, tiled=True)
        all_down = all_down.reshape(parts, heads, slice_rows, down.shape[1])

        image_fourth = lax.dynamic_slice_in_dim(image, parallel_index * fourth, fourth, 1)
        low = jnp.dot(image_fourth, down, preferred_element_type=f32)
        low = lax.all_gather(low, "mp", axis=0)
        low = jnp.sum(low, axis=0).astype(bf16)
        adapted = jnp.concatenate(
            [
                jnp.dot(low[:, :lowrank], up_key, preferred_element_type=f32),
                jnp.dot(low[:, lowrank:], up_value, preferred_element_type=f32),
            ],
            axis=1,
        )
        key_value = (jnp.dot(image, weight, preferred_element_type=f32) + adapter_scale * adapted).astype(bf16)

        local_kv = columns // HD
        text_rows = queries.shape[2]
        group = queries.shape[3] // HD // local_kv
        query_rows = queries[0, 0].reshape(text_rows, local_kv, group, HD)
        cot_rows = cotangent[0, 0].reshape(text_rows, local_kv, group, HD)
        key_rows = key_value[:, :columns].reshape(rows, local_kv, HD)
        value_rows = key_value[:, columns:].reshape(rows, local_kv, HD)
        key_mask = position < image_tile_count[0] * (rows // TILES)
        row_mask = (jnp.arange(text_rows, dtype=jnp.int32) < text_token_length[0]).astype(f32)
        scores = jnp.einsum("tgrd,jgd->grtj", query_rows, key_rows, preferred_element_type=f32) * HD ** (-0.5)
        masked = jnp.where(key_mask[None, None, None, :], scores, -1e30)
        row_top = jnp.max(masked, axis=-1, keepdims=True)
        shifted = jnp.exp(masked - row_top)
        attention = shifted / jnp.sum(shifted, axis=-1, keepdims=True)
        row_gate = row_mask[None, None, :, None]
        kept = attention.astype(bf16) * row_gate.astype(bf16)
        dweights = jnp.einsum("tgrd,jgd->grtj", cot_rows, value_rows, preferred_element_type=f32)
        row_delta = jnp.sum(attention * dweights, axis=-1, keepdims=True)
        dscore = (attention * (dweights - row_delta) * row_gate * HD ** (-0.5)).astype(bf16)
        key_grad = jnp.einsum("grtj,tgrd->jgd", dscore, query_rows, preferred_element_type=f32)
        value_grad = jnp.einsum("grtj,tgrd->jgd", kept, cot_rows, preferred_element_type=f32)
        kv_grad = jnp.concatenate(
            [key_grad.reshape(rows, columns), value_grad.reshape(rows, columns)], axis=1
        ).astype(bf16)

        back = adapter_scale * jnp.concatenate(
            [
                lax.dot_general(kv_grad[:, :columns], up_key, contracted_columns, preferred_element_type=f32),
                lax.dot_general(kv_grad[:, columns:], up_value, contracted_columns, preferred_element_type=f32),
            ],
            axis=1,
        )

        stay, next_x, far_x, prior_x = image_grad_blocks(kv_grad, back.astype(bf16), weight, all_down)
        image_grad = (
            stay
            + shift(next_x, dx=1).astype(f32)
            + shift(far_x, dx=2, opposite=True).astype(f32)
            + shift(prior_x, dx=-1).astype(f32)
        )

        back = lax.all_gather(back, "mp", axis=0)
        back = jnp.sum(back, axis=0).astype(bf16)
        down_grad = lax.dot_general(image_fourth, back, contract_rows, preferred_element_type=f32)
        up_grad = adapter_scale * jnp.stack(
            [
                lax.dot_general(low[:, :lowrank], kv_grad[:, :columns], contract_rows, preferred_element_type=f32),
                lax.dot_general(low[:, lowrank:], kv_grad[:, columns:], contract_rows, preferred_element_type=f32),
            ]
        )
        both = jnp.concatenate([down_grad, up_grad.reshape(-1, down_grad.shape[1])], axis=0)
        both = lax.psum_scatter(both, "dp", scatter_dimension=0, tiled=True)
        both = both.astype(bf16)

        send = image_grad[tokens:].astype(bf16)
        image_grad = (
            image_grad[:tokens]
            + shift(send[:tokens], dz=1).astype(f32)
            + shift(send[tokens : 2 * tokens], dz=2, opposite=True).astype(f32)
            + shift(send[2 * tokens :], dz=-1).astype(f32)
        )
        result = sum_over_mp(image_grad.astype(bf16), f32)
        both = lax.all_gather(both, "dp", axis=0, tiled=True)
        down_out = both[:fourth]
        up_out = both[fourth:].reshape(up_grad.shape)
        return (down_out[None], up_out[None], result[None])

    return body


def solution(mesh):
    in_specs = (
        P("dp", "segment", None),
        P("segment", "dp", None, "mp"),
        P("segment", "mp", None),
        P("segment", None, None, "mp"),
        P("segment", "dp", None, "mp"),
        P("segment", "dp", None, "mp"),
        P("dp"),
        P("dp"),
    )
    out_specs = (P("segment", "mp", None), P("segment", None, None, "mp"), P("dp", "segment", None))
    body = make_body(mesh)

    return jax.shard_map(body, mesh=mesh, in_specs=in_specs, out_specs=out_specs, check_vma=False)
```

```python
import jax
import jax.numpy as jnp
from jax import lax
from jax.experimental import pallas as pl
from jax.experimental.pallas import tpu as pltpu
from jax.sharding import PartitionSpec as P


HD = 128
TILES = 4
SIDE = 4
CORES = 2

adapter_scale = 2.0
contract_rows = (((0,), (0,)), ((), ()))
contracted_columns = (((1,), (1,)), ((), ()))
f32 = jnp.float32
bf16 = jnp.bfloat16
AXES = ("segment", "dp", "mp")


def layer_kernel(
    image_ref,
    weight_ref,
    low_ref,
    up_ref,
    query_ref,
    cot_ref,
    valid_ref,
    live_ref,
    kv_grad_ref,
    back_ref,
    own_ref,
    *rest,
):
    *away_refs, sum_ref = rest
    step = pl.program_id(0)
    forward_steps = pl.num_programs(0) // 2
    columns = weight_ref.shape[1] // 2
    local_kv = columns // HD
    group = query_ref.shape[1] // HD // local_kv
    block = own_ref.shape[0]

    @pl.when(step < forward_steps)
    def _():
        part = jnp.dot(image_ref[...], weight_ref[...], preferred_element_type=f32)

        @pl.when(step == 0)
        def _():
            sum_ref[...] = part

        @pl.when(step > 0)
        def _():
            sum_ref[...] += part

    @pl.when(step == forward_steps - 1)
    def _():
        adapted = jnp.dot(low_ref[...], up_ref[...], preferred_element_type=f32)
        key_value = (sum_ref[...] + adapter_scale * adapted).astype(bf16)
        valid = valid_ref[...] > 0
        live = live_ref[0:1, :]
        for g in range(local_kv):
            key_at, value_at = g * HD, columns + g * HD
            keys = key_value[:, key_at : key_at + HD]
            values = key_value[:, value_at : value_at + HD]
            key_grad = value_grad = None
            for r in range(group):
                at = (g * group + r) * HD
                query, cot = query_ref[:, at : at + HD], cot_ref[:, at : at + HD]
                scores = lax.dot_general(keys, query, contracted_columns, preferred_element_type=f32) * HD ** (-0.5)
                masked = jnp.where(valid, scores, -1e30)
                shifted = jnp.exp(masked - jnp.max(masked, axis=0, keepdims=True))
                attention = shifted * (1.0 / jnp.sum(shifted, axis=0, keepdims=True))
                dweights = lax.dot_general(values, cot, contracted_columns, preferred_element_type=f32)
                delta = jnp.sum(attention * dweights, axis=0, keepdims=True)
                dscore = (attention * (dweights - delta) * (live * HD ** (-0.5))).astype(bf16)
                kept = (attention * live).astype(bf16)
                dk = jnp.dot(dscore, query, preferred_element_type=f32)
                dv = jnp.dot(kept, cot, preferred_element_type=f32)
                key_grad = dk if r == 0 else key_grad + dk
                value_grad = dv if r == 0 else value_grad + dv
            kv_grad_ref[:, key_at : key_at + HD] = key_grad.astype(bf16)
            kv_grad_ref[:, value_at : value_at + HD] = value_grad.astype(bf16)
        back_ref[...] = adapter_scale * lax.dot_general(
            kv_grad_ref[...], up_ref[...], contracted_columns, preferred_element_type=f32
        )

    @pl.when(step >= forward_steps)
    def _():
        total = lax.dot_general(kv_grad_ref[...], weight_ref[...], contracted_columns, preferred_element_type=f32)
        own_ref[...] = total[:block]
        for i, ref in enumerate(away_refs):
            ref[...] = total[(i + 1) * block : (i + 2) * block].astype(bf16)


def layer(image, weight, low, up, query, cot, valid, live):
    rows, width = image.shape
    columns = weight.shape[1]
    rank = low.shape[1]
    steps = 8
    share = width // steps
    block = rows // SIDE

    def whole(v):
        return pl.BlockSpec(v.shape, lambda j: (0, 0))

    def turn(j):
        return jnp.minimum(j, 2 * steps - 1 - j)

    out_spec = pl.BlockSpec((block, share), lambda j: (0, jnp.minimum(steps - 1, 2 * steps - 1 - j)))
    return pl.pallas_call(
        layer_kernel,
        grid=(2 * steps,),
        in_specs=[
            pl.BlockSpec((rows, share), lambda j: (0, jnp.minimum(j, steps - 1))),
            pl.BlockSpec((share, columns), lambda j: (turn(j), 0)),
            whole(low),
            whole(up),
            whole(query),
            whole(cot),
            whole(valid),
            whole(live),
        ],
        out_specs=[
            pl.BlockSpec((rows, columns), lambda j: (0, 0)),
            pl.BlockSpec((rows, rank), lambda j: (0, 0)),
        ]
        + [out_spec] * SIDE,
        out_shape=[
            jax.ShapeDtypeStruct((rows, columns), bf16),
            jax.ShapeDtypeStruct((rows, rank), f32),
            jax.ShapeDtypeStruct((block, width), f32),
        ]
        + [jax.ShapeDtypeStruct((block, width), bf16)] * (SIDE - 1),
        scratch_shapes=[pltpu.VMEM((rows, columns), f32)],
        name="layer",
    )(image, weight, low, up, query, cot, valid, live)


def make_body(mesh):
    segments, parts, heads = (mesh.shape[a] for a in AXES)
    runs = segments // SIDE
    ring = runs * heads

    def shift(v, dx=0, dz=0, opposite=False):
        pairs = []
        for s in range(segments):
            for d in range(parts):
                for m in range(heads):
                    z_lo, x = divmod(s, SIDE)
                    sign = -1 if (opposite and d % CORES) else 1
                    x2 = (x + sign * dx) % SIDE
                    m2, z2 = divmod((m * runs + z_lo + sign * dz) % ring, runs)
                    pairs.append(((s * parts + d) * heads + m, ((z2 * SIDE + x2) * parts + d) * heads + m2))
        return lax.ppermute(v, AXES, pairs)

    def sum_over_mp(v, out):
        far = shift(v, dz=2 * runs, opposite=True)
        near = shift(v, dz=runs)
        prior = shift(v, dz=-runs)
        return ((v.astype(f32) + far.astype(f32)) + (near.astype(f32) + prior.astype(f32))).astype(out)

    def body(
        encoder_image_states,
        frozen_key_value,
        adapter_down_weight,
        adapter_up_weight,
        queries,
        cotangent,
        text_token_length,
        image_tile_count,
    ):
        own = encoder_image_states[0]
        tokens, _ = own.shape
        parallel_index = lax.axis_index("mp")
        segment_index = lax.axis_index("segment")
        lowrank, columns = adapter_up_weight.shape[2:]
        up_key, up_value = adapter_up_weight[0, 0], adapter_up_weight[0, 1]
        down = adapter_down_weight[0]
        fourth = down.shape[0]

        line = [shift(own, dz=-1), shift(own, dz=2, opposite=True), shift(own, dz=1)]
        others = jnp.concatenate(line, axis=0)
        image = jnp.concatenate(
            [
                own,
                *line,
                shift(own, dx=-1),
                shift(others, dx=-1),
                shift(own, dx=2, opposite=True),
                shift(others, dx=2, opposite=True),
                shift(own, dx=1),
                shift(others, dx=1),
            ],
            axis=0,
        )
        rows = image.shape[0]
        offset = jnp.arange(rows, dtype=jnp.int32)
        x_off, z_off, tok = offset // (runs * tokens), (offset // tokens) % runs, offset % tokens
        position = (
            ((segment_index // SIDE + z_off) % runs) * SIDE + (segment_index % SIDE + x_off) % SIDE
        ) * tokens + tok

        local_weight = frozen_key_value[0].reshape(-1, CORES * columns)
        weight = lax.all_gather(local_weight, "dp", axis=0, tiled=True)
        image_fourth = lax.dynamic_slice_in_dim(image, parallel_index * fourth, fourth, 1)
        low = jnp.dot(image_fourth, down, preferred_element_type=f32)
        low = lax.all_gather(low, "mp", axis=0)
        low = jnp.sum(low, axis=0).astype(bf16)
        text_rows = queries.shape[2]
        none = jnp.zeros_like(up_key)
        up_both = jnp.concatenate(
            [jnp.concatenate([up_key, none], axis=1), jnp.concatenate([none, up_value], axis=1)], axis=0
        )
        valid = (position < image_tile_count[0] * (rows // TILES)).astype(f32)
        live = (jnp.arange(text_rows, dtype=jnp.int32) < text_token_length[0]).astype(f32)
        kv_grad, back, stay, next_x, far_x, prior_x = layer(
            image,
            weight,
            low,
            up_both,
            queries[0, 0],
            cotangent[0, 0],
            jnp.broadcast_to(valid[:, None], (rows, text_rows)),
            jnp.broadcast_to(live[None, :], (8, text_rows)),
        )

        image_grad = (
            stay
            + shift(next_x, dx=1).astype(f32)
            + shift(far_x, dx=2, opposite=True).astype(f32)
            + shift(prior_x, dx=-1).astype(f32)
        )

        back = lax.all_gather(back, "mp", axis=0)
        back = jnp.sum(back, axis=0).astype(bf16)
        adapter_grad = lax.dot_general(back, down, contracted_columns, preferred_element_type=f32)
        block = stay.shape[0]
        adapter_away = adapter_grad.astype(bf16)
        adapter_grad = (
            adapter_grad[:block]
            + shift(adapter_away[block : 2 * block], dx=1).astype(f32)
            + shift(adapter_away[2 * block : 3 * block], dx=2, opposite=True).astype(f32)
            + shift(adapter_away[3 * block :], dx=-1).astype(f32)
        )
        here = lax.dynamic_slice_in_dim(image_grad, parallel_index * fourth, fourth, 1)
        image_grad = lax.dynamic_update_slice_in_dim(image_grad, here + adapter_grad, parallel_index * fourth, 1)

        down_grad = lax.dot_general(image_fourth, back, contract_rows, preferred_element_type=f32)
        up_grad = adapter_scale * jnp.stack(
            [
                lax.dot_general(low[:, :lowrank], kv_grad[:, :columns], contract_rows, preferred_element_type=f32),
                lax.dot_general(low[:, lowrank:], kv_grad[:, columns:], contract_rows, preferred_element_type=f32),
            ]
        )
        both = jnp.concatenate([down_grad, up_grad.reshape(-1, down_grad.shape[1])], axis=0)
        both = lax.psum_scatter(both, "dp", scatter_dimension=0, tiled=True)
        both = both.astype(bf16)

        send = image_grad[tokens:].astype(bf16)
        image_grad = (
            image_grad[:tokens]
            + shift(send[:tokens], dz=1).astype(f32)
            + shift(send[tokens : 2 * tokens], dz=2, opposite=True).astype(f32)
            + shift(send[2 * tokens :], dz=-1).astype(f32)
        )
        result = sum_over_mp(image_grad.astype(bf16), f32)
        both = lax.all_gather(both, "dp", axis=0, tiled=True)
        down_out = both[:fourth]
        up_out = both[fourth:].reshape(up_grad.shape)
        return (down_out[None], up_out[None], result[None])

    return body


def solution(mesh):
    in_specs = (
        P("dp", "segment", None),
        P("segment", "dp", None, "mp"),
        P("segment", "mp", None),
        P("segment", None, None, "mp"),
        P("segment", "dp", None, "mp"),
        P("segment", "dp", None, "mp"),
        P("dp"),
        P("dp"),
    )
    out_specs = (P("segment", "mp", None), P("segment", None, None, "mp"), P("dp", "segment", None))
    body = make_body(mesh)

    return jax.shard_map(body, mesh=mesh, in_specs=in_specs, out_specs=out_specs, check_vma=False)
```

```python
import jax
import jax.numpy as jnp
from jax import lax
from jax.experimental import pallas as pl
from jax.experimental.pallas import tpu as pltpu
from jax.sharding import PartitionSpec as P


HD = 128
TILES = 4
SIDE = 4
CORES = 2

adapter_scale = 2.0
contract_rows = (((0,), (0,)), ((), ()))
contracted_columns = (((1,), (1,)), ((), ()))
f32 = jnp.float32
bf16 = jnp.bfloat16
AXES = ("segment", "dp", "mp")


CHUNKS = 8


def layer_kernel(
    image_hbm,
    weight_hbm,
    query_hbm,
    cot_hbm,
    low_ref,
    up_ref,
    valid_ref,
    live_ref,
    kv_grad_ref,
    back_ref,
    own_ref,
    *rest,
):
    *away_refs, image_ref, weight_ref, query_ref, cot_ref, sems = rest
    columns = weight_ref.shape[1] // 2
    local_kv = columns // HD
    group = query_ref.shape[1] // HD // local_kv
    block = own_ref.shape[0]
    share = weight_ref.shape[0] // CHUNKS

    def chunk(c):
        return pl.ds(c * share, share)

    image_copy = pltpu.make_async_copy(image_hbm, image_ref, sems.at[CHUNKS])
    query_copy = pltpu.make_async_copy(query_hbm, query_ref, sems.at[CHUNKS + 1])
    cot_copy = pltpu.make_async_copy(cot_hbm, cot_ref, sems.at[CHUNKS + 2])
    weight_copies = [
        pltpu.make_async_copy(weight_hbm.at[chunk(c)], weight_ref.at[chunk(c)], sems.at[c]) for c in range(CHUNKS)
    ]
    image_copy.start()
    for copy in weight_copies:
        copy.start()
    query_copy.start()
    cot_copy.start()

    key_value = adapter_scale * jnp.dot(low_ref[...], up_ref[...], preferred_element_type=f32)
    image_copy.wait()
    for c, copy in enumerate(weight_copies):
        copy.wait()
        key_value += jnp.dot(image_ref[:, chunk(c)], weight_ref[chunk(c), :], preferred_element_type=f32)
    key_value = key_value.astype(bf16)
    query_copy.wait()
    cot_copy.wait()
    valid = valid_ref[...] > 0
    live = live_ref[0:1, :]
    for g in range(local_kv):
        key_at, value_at = g * HD, columns + g * HD
        keys = key_value[:, key_at : key_at + HD]
        values = key_value[:, value_at : value_at + HD]
        key_grad = value_grad = None
        for r in range(group):
            at = (g * group + r) * HD
            query, cot = query_ref[:, at : at + HD], cot_ref[:, at : at + HD]
            scores = lax.dot_general(keys, query, contracted_columns, preferred_element_type=f32) * HD ** (-0.5)
            masked = jnp.where(valid, scores, -1e30)
            shifted = jnp.exp(masked - jnp.max(masked, axis=0, keepdims=True))
            attention = shifted * (1.0 / jnp.sum(shifted, axis=0, keepdims=True))
            dweights = lax.dot_general(values, cot, contracted_columns, preferred_element_type=f32)
            delta = jnp.sum(attention * dweights, axis=0, keepdims=True)
            dscore = (attention * (dweights - delta) * (live * HD ** (-0.5))).astype(bf16)
            kept = (attention * live).astype(bf16)
            dk = jnp.dot(dscore, query, preferred_element_type=f32)
            dv = jnp.dot(kept, cot, preferred_element_type=f32)
            key_grad = dk if r == 0 else key_grad + dk
            value_grad = dv if r == 0 else value_grad + dv
        kv_grad_ref[:, key_at : key_at + HD] = key_grad.astype(bf16)
        kv_grad_ref[:, value_at : value_at + HD] = value_grad.astype(bf16)
    kv_grad = kv_grad_ref[...]
    back = adapter_scale * lax.dot_general(kv_grad, up_ref[...], contracted_columns, preferred_element_type=f32)
    back_ref[...] = back.astype(bf16)
    for c in range(CHUNKS):
        total = lax.dot_general(kv_grad, weight_ref[chunk(c), :], contracted_columns, preferred_element_type=f32)
        own_ref[:, chunk(c)] = total[:block]
        for i, ref in enumerate(away_refs):
            ref[:, chunk(c)] = total[(i + 1) * block : (i + 2) * block].astype(bf16)


def layer(image, weight, low, up, query, cot, valid, live):
    rows, width = image.shape
    columns = weight.shape[1]
    rank = low.shape[1]
    block = rows // SIDE
    outside = pl.BlockSpec(memory_space=pl.ANY)
    inside_vmem = pl.BlockSpec(memory_space=pltpu.VMEM)
    return pl.pallas_call(
        layer_kernel,
        in_specs=[outside] * 4 + [inside_vmem] * 4,
        out_specs=[inside_vmem] * (2 + SIDE),
        out_shape=[
            jax.ShapeDtypeStruct((rows, columns), bf16),
            jax.ShapeDtypeStruct((rows, rank), bf16),
            jax.ShapeDtypeStruct((block, width), f32),
        ]
        + [jax.ShapeDtypeStruct((block, width), bf16)] * (SIDE - 1),
        scratch_shapes=[
            pltpu.VMEM(image.shape, bf16),
            pltpu.VMEM(weight.shape, bf16),
            pltpu.VMEM(query.shape, bf16),
            pltpu.VMEM(cot.shape, bf16),
            pltpu.SemaphoreType.DMA((CHUNKS + 3,)),
        ],
        name="layer",
    )(image, weight, query, cot, low, up, valid, live)


def make_body(mesh):
    segments, parts, heads = (mesh.shape[a] for a in AXES)
    runs = segments // SIDE
    ring = runs * heads

    def shift(v, dx=0, dz=0, opposite=False):
        pairs = []
        for s in range(segments):
            for d in range(parts):
                for m in range(heads):
                    z_lo, x = divmod(s, SIDE)
                    sign = -1 if (opposite and d % CORES) else 1
                    x2 = (x + sign * dx) % SIDE
                    m2, z2 = divmod((m * runs + z_lo + sign * dz) % ring, runs)
                    pairs.append(((s * parts + d) * heads + m, ((z2 * SIDE + x2) * parts + d) * heads + m2))
        return lax.ppermute(v, AXES, pairs)

    def sum_over_mp(v, out):
        far = shift(v, dz=2 * runs, opposite=True)
        near = shift(v, dz=runs)
        prior = shift(v, dz=-runs)
        return ((v.astype(f32) + far.astype(f32)) + (near.astype(f32) + prior.astype(f32))).astype(out)

    def body(
        encoder_image_states,
        frozen_key_value,
        adapter_down_weight,
        adapter_up_weight,
        queries,
        cotangent,
        text_token_length,
        image_tile_count,
    ):
        own = encoder_image_states[0]
        tokens, _ = own.shape
        parallel_index = lax.axis_index("mp")
        segment_index = lax.axis_index("segment")
        lowrank, columns = adapter_up_weight.shape[2:]
        up_key, up_value = adapter_up_weight[0, 0], adapter_up_weight[0, 1]
        down = adapter_down_weight[0]
        fourth = down.shape[0]

        line = [shift(own, dz=-1), shift(own, dz=2, opposite=True), shift(own, dz=1)]
        others = jnp.concatenate(line, axis=0)
        image = jnp.concatenate(
            [
                own,
                *line,
                shift(own, dx=-1),
                shift(others, dx=-1),
                shift(own, dx=2, opposite=True),
                shift(others, dx=2, opposite=True),
                shift(own, dx=1),
                shift(others, dx=1),
            ],
            axis=0,
        )
        rows = image.shape[0]
        offset = jnp.arange(rows, dtype=jnp.int32)
        x_off, z_off, tok = offset // (runs * tokens), (offset // tokens) % runs, offset % tokens
        position = (
            ((segment_index // SIDE + z_off) % runs) * SIDE + (segment_index % SIDE + x_off) % SIDE
        ) * tokens + tok

        local_weight = frozen_key_value[0].reshape(-1, CORES * columns)
        weight = lax.all_gather(local_weight, "dp", axis=0, tiled=True)
        image_fourth = lax.dynamic_slice_in_dim(image, parallel_index * fourth, fourth, 1)
        low = jnp.dot(image_fourth, down, preferred_element_type=f32)
        low = lax.all_gather(low, "mp", axis=0)
        low = jnp.sum(low, axis=0).astype(bf16)
        text_rows = queries.shape[2]
        none = jnp.zeros_like(up_key)
        up_both = jnp.concatenate(
            [jnp.concatenate([up_key, none], axis=1), jnp.concatenate([none, up_value], axis=1)], axis=0
        )
        valid = (position < image_tile_count[0] * (rows // TILES)).astype(f32)
        live = (jnp.arange(text_rows, dtype=jnp.int32) < text_token_length[0]).astype(f32)
        valid = jnp.broadcast_to(valid[:, None], (rows, text_rows))
        live = jnp.broadcast_to(live[None, :], (8, text_rows))
        kv_grad, back, stay, next_x, far_x, prior_x = layer(
            image,
            weight,
            low,
            up_both,
            queries[0, 0],
            cotangent[0, 0],
            valid,
            live,
        )

        image_grad = (
            stay
            + shift(next_x, dx=1).astype(f32)
            + shift(far_x, dx=2, opposite=True).astype(f32)
            + shift(prior_x, dx=-1).astype(f32)
        )

        back = lax.all_gather(back, "mp", axis=0)
        back = jnp.sum(back.astype(f32), axis=0).astype(bf16)
        adapter_grad = lax.dot_general(back, down, contracted_columns, preferred_element_type=f32)
        block = stay.shape[0]
        adapter_away = adapter_grad.astype(bf16)
        adapter_grad = (
            adapter_grad[:block]
            + shift(adapter_away[block : 2 * block], dx=1).astype(f32)
            + shift(adapter_away[2 * block : 3 * block], dx=2, opposite=True).astype(f32)
            + shift(adapter_away[3 * block :], dx=-1).astype(f32)
        )
        here = lax.dynamic_slice_in_dim(image_grad, parallel_index * fourth, fourth, 1)
        image_grad = lax.dynamic_update_slice_in_dim(image_grad, here + adapter_grad, parallel_index * fourth, 1)

        down_grad = lax.dot_general(image_fourth, back, contract_rows, preferred_element_type=f32)
        up_grad = adapter_scale * jnp.stack(
            [
                lax.dot_general(low[:, :lowrank], kv_grad[:, :columns], contract_rows, preferred_element_type=f32),
                lax.dot_general(low[:, lowrank:], kv_grad[:, columns:], contract_rows, preferred_element_type=f32),
            ]
        )
        both = jnp.concatenate([down_grad, up_grad.reshape(-1, down_grad.shape[1])], axis=0)
        both = lax.psum_scatter(both, "dp", scatter_dimension=0, tiled=True)
        both = both.astype(bf16)

        send = image_grad[tokens:].astype(bf16)
        image_grad = (
            image_grad[:tokens]
            + shift(send[:tokens], dz=1).astype(f32)
            + shift(send[tokens : 2 * tokens], dz=2, opposite=True).astype(f32)
            + shift(send[2 * tokens :], dz=-1).astype(f32)
        )
        result = sum_over_mp(image_grad.astype(bf16), f32)
        both = lax.all_gather(both, "dp", axis=0, tiled=True)
        down_out = both[:fourth]
        up_out = both[fourth:].reshape(up_grad.shape)
        return (down_out[None], up_out[None], result[None])

    return body


def solution(mesh):
    in_specs = (
        P("dp", "segment", None),
        P("segment", "dp", None, "mp"),
        P("segment", "mp", None),
        P("segment", None, None, "mp"),
        P("segment", "dp", None, "mp"),
        P("segment", "dp", None, "mp"),
        P("dp"),
        P("dp"),
    )
    out_specs = (P("segment", "mp", None), P("segment", None, None, "mp"), P("dp", "segment", None))
    body = make_body(mesh)

    return jax.shard_map(body, mesh=mesh, in_specs=in_specs, out_specs=out_specs, check_vma=False)
```

```python
import jax
import jax.numpy as jnp
from jax import lax
from jax.experimental import pallas as pl
from jax.experimental.pallas import tpu as pltpu
from jax.sharding import PartitionSpec as P


HD = 128
TILES = 4
SIDE = 4
CORES = 2

adapter_scale = 2.0
contract_rows = (((0,), (0,)), ((), ()))
contracted_columns = (((1,), (1,)), ((), ()))
f32 = jnp.float32
bf16 = jnp.bfloat16
AXES = ("segment", "dp", "mp")


CHUNKS = 8


def layer_kernel(*refs):
    pieces, refs = refs[: 2 * SIDE], refs[2 * SIDE :]
    weight_hbm, query_hbm, cot_hbm, head_ref, low_ref, up_ref, valid_ref, live_ref, *refs = refs
    kv_grad_ref, back_ref, own_ref, *rest = refs
    *away_refs, quarter_ref, others_ref, weight_ref, query_ref, cot_ref, sems = rest
    columns = weight_ref.shape[1] // 2
    local_kv = columns // HD
    group = query_ref.shape[1] // HD // local_kv
    block = own_ref.shape[0]
    share = weight_ref.shape[0] // CHUNKS

    first = quarter_ref.shape[1] // share

    def chunk(c):
        return pl.ds(c * share, share)

    def turned(c):
        return pl.ds(pl.multiple_of((head_ref[0] * first + c) % CHUNKS * share, share), share)

    query_copy = pltpu.make_async_copy(query_hbm, query_ref, sems.at[CHUNKS])
    cot_copy = pltpu.make_async_copy(cot_hbm, cot_ref, sems.at[CHUNKS + 1])
    image_copies = []
    for i, piece in enumerate(pieces):
        target = (quarter_ref if i < SIDE else others_ref).at[pl.ds(i % SIDE * block, block)]
        image_copies.append(pltpu.make_async_copy(piece, target, sems.at[CHUNKS + 2 + i]))
    weight_copies = [
        pltpu.make_async_copy(weight_hbm.at[turned(c)], weight_ref.at[turned(c)], sems.at[c]) for c in range(CHUNKS)
    ]
    for copy in image_copies:
        copy.start()
    for copy in weight_copies:
        copy.start()
    query_copy.start()
    cot_copy.start()

    key_value = adapter_scale * jnp.dot(low_ref[...], up_ref[...], preferred_element_type=f32)
    for copy in image_copies:
        copy.wait()
    for c, copy in enumerate(weight_copies):
        copy.wait()
        image = quarter_ref[:, chunk(c)] if c < first else others_ref[:, chunk(c - first)]
        key_value += jnp.dot(image, weight_ref[turned(c), :], preferred_element_type=f32)
    key_value = key_value.astype(bf16)
    query_copy.wait()
    cot_copy.wait()
    valid = valid_ref[...] > 0
    live = live_ref[0:1, :]
    for g in range(local_kv):
        key_at, value_at = g * HD, columns + g * HD
        keys = key_value[:, key_at : key_at + HD]
        values = key_value[:, value_at : value_at + HD]
        key_grad = value_grad = None
        for r in range(group):
            at = (g * group + r) * HD
            query, cot = query_ref[:, at : at + HD], cot_ref[:, at : at + HD]
            scores = lax.dot_general(keys, query, contracted_columns, preferred_element_type=f32) * HD ** (-0.5)
            masked = jnp.where(valid, scores, -1e30)
            shifted = jnp.exp(masked - jnp.max(masked, axis=0, keepdims=True))
            attention = shifted * (1.0 / jnp.sum(shifted, axis=0, keepdims=True))
            dweights = lax.dot_general(values, cot, contracted_columns, preferred_element_type=f32)
            delta = jnp.sum(attention * dweights, axis=0, keepdims=True)
            dscore = (attention * (dweights - delta) * (live * HD ** (-0.5))).astype(bf16)
            kept = (attention * live).astype(bf16)
            dk = jnp.dot(dscore, query, preferred_element_type=f32)
            dv = jnp.dot(kept, cot, preferred_element_type=f32)
            key_grad = dk if r == 0 else key_grad + dk
            value_grad = dv if r == 0 else value_grad + dv
        kv_grad_ref[:, key_at : key_at + HD] = key_grad.astype(bf16)
        kv_grad_ref[:, value_at : value_at + HD] = value_grad.astype(bf16)
    kv_grad = kv_grad_ref[...]
    back = adapter_scale * lax.dot_general(kv_grad, up_ref[...], contracted_columns, preferred_element_type=f32)
    back_ref[...] = back.astype(bf16)
    for c in range(CHUNKS):
        total = lax.dot_general(kv_grad, weight_ref[chunk(c), :], contracted_columns, preferred_element_type=f32)
        own_ref[:, chunk(c)] = total[:block]
        for i, ref in enumerate(away_refs):
            ref[:, chunk(c)] = total[(i + 1) * block : (i + 2) * block].astype(bf16)


def layer(quarter, others, weight, head, low, up, query, cot, valid, live):
    rows, width = SIDE * quarter[0].shape[0], weight.shape[0]
    columns = weight.shape[1]
    rank = low.shape[1]
    block = rows // SIDE
    outside = pl.BlockSpec(memory_space=pl.ANY)
    inside_vmem = pl.BlockSpec(memory_space=pltpu.VMEM)
    return pl.pallas_call(
        layer_kernel,
        in_specs=[outside] * (2 * SIDE + 3) + [pl.BlockSpec(memory_space=pltpu.SMEM)] + [inside_vmem] * 4,
        out_specs=[inside_vmem] * (2 + SIDE),
        out_shape=[
            jax.ShapeDtypeStruct((rows, columns), bf16),
            jax.ShapeDtypeStruct((rows, rank), bf16),
            jax.ShapeDtypeStruct((block, width), f32),
        ]
        + [jax.ShapeDtypeStruct((block, width), bf16)] * (SIDE - 1),
        scratch_shapes=[
            pltpu.VMEM((rows, quarter[0].shape[1]), bf16),
            pltpu.VMEM((rows, others[0].shape[1]), bf16),
            pltpu.VMEM(weight.shape, bf16),
            pltpu.VMEM(query.shape, bf16),
            pltpu.VMEM(cot.shape, bf16),
            pltpu.SemaphoreType.DMA((CHUNKS + 2 + 2 * SIDE,)),
        ],
        name="layer",
    )(*quarter, *others, weight, query, cot, head, low, up, valid, live)


def make_body(mesh):
    segments, parts, heads = (mesh.shape[a] for a in AXES)
    runs = segments // SIDE
    ring = runs * heads

    def shift(v, dx=0, dz=0, opposite=False):
        pairs = []
        for s in range(segments):
            for d in range(parts):
                for m in range(heads):
                    z_lo, x = divmod(s, SIDE)
                    sign = -1 if (opposite and d % CORES) else 1
                    x2 = (x + sign * dx) % SIDE
                    m2, z2 = divmod((m * runs + z_lo + sign * dz) % ring, runs)
                    pairs.append(((s * parts + d) * heads + m, ((z2 * SIDE + x2) * parts + d) * heads + m2))
        return lax.ppermute(v, AXES, pairs)

    def sum_over_mp(v, out):
        far = shift(v, dz=2 * runs, opposite=True)
        near = shift(v, dz=runs)
        prior = shift(v, dz=-runs)
        return ((v.astype(f32) + far.astype(f32)) + (near.astype(f32) + prior.astype(f32))).astype(out)

    def body(
        encoder_image_states,
        frozen_key_value,
        adapter_down_weight,
        adapter_up_weight,
        queries,
        cotangent,
        text_token_length,
        image_tile_count,
    ):
        own = encoder_image_states[0]
        tokens, _ = own.shape
        parallel_index = lax.axis_index("mp")
        segment_index = lax.axis_index("segment")
        lowrank, columns = adapter_up_weight.shape[2:]
        up_key, up_value = adapter_up_weight[0, 0], adapter_up_weight[0, 1]
        down = adapter_down_weight[0]
        fourth = down.shape[0]

        line = jnp.concatenate([own, shift(own, dz=-1), shift(own, dz=2, opposite=True), shift(own, dz=1)], axis=0)

        def quarter_of(k):
            return lax.dynamic_slice_in_dim(line, (parallel_index + k) % heads * fourth, fourth, 1)

        def over_line(v):
            return [v, shift(v, dx=-1), shift(v, dx=2, opposite=True), shift(v, dx=1)]

        quarter = over_line(quarter_of(0))
        image_fourth = jnp.concatenate(quarter, axis=0)
        image_others = over_line(jnp.concatenate([quarter_of(k) for k in range(1, heads)], axis=1))
        rows = image_fourth.shape[0]
        offset = jnp.arange(rows, dtype=jnp.int32)
        x_off, z_off, tok = offset // (runs * tokens), (offset // tokens) % runs, offset % tokens
        position = (
            ((segment_index // SIDE + z_off) % runs) * SIDE + (segment_index % SIDE + x_off) % SIDE
        ) * tokens + tok

        local_weight = frozen_key_value[0].reshape(-1, CORES * columns)
        weight = lax.all_gather(local_weight, "dp", axis=0, tiled=True)
        low = jnp.dot(image_fourth, down, preferred_element_type=f32)
        low = lax.all_gather(low, "mp", axis=0)
        low = jnp.sum(low, axis=0).astype(bf16)
        text_rows = queries.shape[2]
        none = jnp.zeros_like(up_key)
        up_both = jnp.concatenate(
            [jnp.concatenate([up_key, none], axis=1), jnp.concatenate([none, up_value], axis=1)], axis=0
        )
        valid = (position < image_tile_count[0] * (rows // TILES)).astype(f32)
        live = (jnp.arange(text_rows, dtype=jnp.int32) < text_token_length[0]).astype(f32)
        valid = jnp.broadcast_to(valid[:, None], (rows, text_rows))
        live = jnp.broadcast_to(live[None, :], (8, text_rows))
        kv_grad, back, stay, next_x, far_x, prior_x = layer(
            quarter,
            image_others,
            weight,
            parallel_index.astype(jnp.int32)[None],
            low,
            up_both,
            queries[0, 0],
            cotangent[0, 0],
            valid,
            live,
        )

        image_grad = (
            stay
            + shift(next_x, dx=1).astype(f32)
            + shift(far_x, dx=2, opposite=True).astype(f32)
            + shift(prior_x, dx=-1).astype(f32)
        )

        back = lax.all_gather(back, "mp", axis=0)
        back = jnp.sum(back.astype(f32), axis=0).astype(bf16)
        adapter_grad = lax.dot_general(back, down, contracted_columns, preferred_element_type=f32)
        block = stay.shape[0]
        adapter_away = adapter_grad.astype(bf16)
        adapter_grad = (
            adapter_grad[:block]
            + shift(adapter_away[block : 2 * block], dx=1).astype(f32)
            + shift(adapter_away[2 * block : 3 * block], dx=2, opposite=True).astype(f32)
            + shift(adapter_away[3 * block :], dx=-1).astype(f32)
        )
        here = lax.dynamic_slice_in_dim(image_grad, parallel_index * fourth, fourth, 1)
        image_grad = lax.dynamic_update_slice_in_dim(image_grad, here + adapter_grad, parallel_index * fourth, 1)

        down_grad = lax.dot_general(image_fourth, back, contract_rows, preferred_element_type=f32)
        up_grad = adapter_scale * jnp.stack(
            [
                lax.dot_general(low[:, :lowrank], kv_grad[:, :columns], contract_rows, preferred_element_type=f32),
                lax.dot_general(low[:, lowrank:], kv_grad[:, columns:], contract_rows, preferred_element_type=f32),
            ]
        )
        both = jnp.concatenate([down_grad, up_grad.reshape(-1, down_grad.shape[1])], axis=0)
        both = lax.psum_scatter(both, "dp", scatter_dimension=0, tiled=True)
        both = both.astype(bf16)

        send = image_grad[tokens:].astype(bf16)
        image_grad = (
            image_grad[:tokens]
            + shift(send[:tokens], dz=1).astype(f32)
            + shift(send[tokens : 2 * tokens], dz=2, opposite=True).astype(f32)
            + shift(send[2 * tokens :], dz=-1).astype(f32)
        )
        result = sum_over_mp(image_grad.astype(bf16), f32)
        both = lax.all_gather(both, "dp", axis=0, tiled=True)
        down_out = both[:fourth]
        up_out = both[fourth:].reshape(up_grad.shape)
        return (down_out[None], up_out[None], result[None])

    return body


def solution(mesh):
    in_specs = (
        P("dp", "segment", None),
        P("segment", "dp", None, "mp"),
        P("segment", "mp", None),
        P("segment", None, None, "mp"),
        P("segment", "dp", None, "mp"),
        P("segment", "dp", None, "mp"),
        P("dp"),
        P("dp"),
    )
    out_specs = (P("segment", "mp", None), P("segment", None, None, "mp"), P("dp", "segment", None))
    body = make_body(mesh)

    return jax.shard_map(body, mesh=mesh, in_specs=in_specs, out_specs=out_specs, check_vma=False)
```

```python
import jax
import jax.numpy as jnp
from jax import lax
from jax.experimental import pallas as pl
from jax.experimental.pallas import tpu as pltpu
from jax.sharding import PartitionSpec as P


HD = 128
TILES = 4
SIDE = 4
CORES = 2

adapter_scale = 2.0
contract_rows = (((0,), (0,)), ((), ()))
contracted_columns = (((1,), (1,)), ((), ()))
f32 = jnp.float32
bf16 = jnp.bfloat16
AXES = ("segment", "dp", "mp")


CHUNKS = 8


def layer_kernel(*refs):
    pieces, refs = refs[: 2 * SIDE], refs[2 * SIDE :]
    weight_hbm, query_hbm, cot_hbm, head_ref, low_ref, up_ref, valid_ref, live_ref, *refs = refs
    kv_grad_ref, back_ref, low_out_ref, *rest = refs
    block_hbm, rest = rest[:SIDE], rest[SIDE:]
    own_ref, *away_refs, quarter_ref, others_ref, weight_ref, query_ref, cot_ref, sems = rest
    columns = weight_ref.shape[1] // 2
    local_kv = columns // HD
    group = query_ref.shape[1] // HD // local_kv
    block = own_ref.shape[0]
    share = weight_ref.shape[0] // CHUNKS

    first = quarter_ref.shape[1] // share

    def chunk(c):
        return pl.ds(c * share, share)

    def turned(c):
        return pl.ds(pl.multiple_of((head_ref[0] * first + c) % CHUNKS * share, share), share)

    query_copy = pltpu.make_async_copy(query_hbm, query_ref, sems.at[CHUNKS])
    cot_copy = pltpu.make_async_copy(cot_hbm, cot_ref, sems.at[CHUNKS + 1])
    image_copies = []
    for i, piece in enumerate(pieces):
        target = (quarter_ref if i < SIDE else others_ref).at[pl.ds(i % SIDE * block, block)]
        image_copies.append(pltpu.make_async_copy(piece, target, sems.at[CHUNKS + 2 + i]))
    weight_copies = [
        pltpu.make_async_copy(weight_hbm.at[turned(c)], weight_ref.at[turned(c)], sems.at[c]) for c in range(CHUNKS)
    ]
    for copy in image_copies:
        copy.start()
    for copy in weight_copies:
        copy.start()
    query_copy.start()
    cot_copy.start()

    rows = low_out_ref.shape[0]
    low = sum(low_ref[pl.ds(i * rows, rows), :] for i in range(low_ref.shape[0] // rows)).astype(bf16)
    low_out_ref[...] = low
    key_value = adapter_scale * jnp.dot(low, up_ref[...], preferred_element_type=f32)
    for copy in image_copies:
        copy.wait()
    for c, copy in enumerate(weight_copies):
        copy.wait()
        image = quarter_ref[:, chunk(c)] if c < first else others_ref[:, chunk(c - first)]
        key_value += jnp.dot(image, weight_ref[turned(c), :], preferred_element_type=f32)
    key_value = key_value.astype(bf16)
    query_copy.wait()
    cot_copy.wait()
    valid = valid_ref[...] > 0
    live = live_ref[0:1, :]
    for g in range(local_kv):
        key_at, value_at = g * HD, columns + g * HD
        keys = key_value[:, key_at : key_at + HD]
        values = key_value[:, value_at : value_at + HD]
        key_grad = value_grad = None
        for r in range(group):
            at = (g * group + r) * HD
            query, cot = query_ref[:, at : at + HD], cot_ref[:, at : at + HD]
            scores = lax.dot_general(keys, query, contracted_columns, preferred_element_type=f32) * HD ** (-0.5)
            masked = jnp.where(valid, scores, -1e30)
            shifted = jnp.exp(masked - jnp.max(masked, axis=0, keepdims=True))
            attention = shifted * (1.0 / jnp.sum(shifted, axis=0, keepdims=True))
            dweights = lax.dot_general(values, cot, contracted_columns, preferred_element_type=f32)
            delta = jnp.sum(attention * dweights, axis=0, keepdims=True)
            dscore = (attention * (dweights - delta) * (live * HD ** (-0.5))).astype(bf16)
            kept = (attention * live).astype(bf16)
            dk = jnp.dot(dscore, query, preferred_element_type=f32)
            dv = jnp.dot(kept, cot, preferred_element_type=f32)
            key_grad = dk if r == 0 else key_grad + dk
            value_grad = dv if r == 0 else value_grad + dv
        kv_grad_ref[:, key_at : key_at + HD] = key_grad.astype(bf16)
        kv_grad_ref[:, value_at : value_at + HD] = value_grad.astype(bf16)
    kv_grad = kv_grad_ref[...]
    back = adapter_scale * lax.dot_general(kv_grad, up_ref[...], contracted_columns, preferred_element_type=f32)
    back_ref[...] = back.astype(bf16)
    out_copies = []
    for c in range(CHUNKS):
        total = lax.dot_general(kv_grad, weight_ref[chunk(c), :], contracted_columns, preferred_element_type=f32)
        own_ref[:, chunk(c)] = total[:block]
        for i, ref in enumerate(away_refs):
            ref[:, chunk(c)] = total[(i + 1) * block : (i + 2) * block].astype(bf16)
        for i, (ref, target) in enumerate(zip((own_ref, *away_refs), block_hbm)):
            copy = pltpu.make_async_copy(
                ref.at[:, chunk(c)], target.at[:, chunk(c)], sems.at[CHUNKS + 2 + 2 * SIDE + c * SIDE + i]
            )
            copy.start()
            out_copies.append(copy)
    for copy in out_copies:
        copy.wait()


def layer(quarter, others, weight, head, low, up, query, cot, valid, live):
    rows, width = SIDE * quarter[0].shape[0], weight.shape[0]
    columns = weight.shape[1]
    rank = low.shape[1]
    block = rows // SIDE
    blocks = [(block, width, f32)] + [(block, width, bf16)] * (SIDE - 1)
    outside = pl.BlockSpec(memory_space=pl.ANY)
    inside_vmem = pl.BlockSpec(memory_space=pltpu.VMEM)
    return pl.pallas_call(
        layer_kernel,
        in_specs=[outside] * (2 * SIDE + 3) + [pl.BlockSpec(memory_space=pltpu.SMEM)] + [inside_vmem] * 4,
        out_specs=[inside_vmem] * 3 + [outside] * SIDE,
        out_shape=[
            jax.ShapeDtypeStruct((rows, columns), bf16),
            jax.ShapeDtypeStruct((rows, rank), bf16),
            jax.ShapeDtypeStruct((rows, rank), bf16),
        ]
        + [jax.ShapeDtypeStruct(v[:2], v[2]) for v in blocks],
        scratch_shapes=[pltpu.VMEM(v[:2], v[2]) for v in blocks]
        + [
            pltpu.VMEM((rows, quarter[0].shape[1]), bf16),
            pltpu.VMEM((rows, others[0].shape[1]), bf16),
            pltpu.VMEM(weight.shape, bf16),
            pltpu.VMEM(query.shape, bf16),
            pltpu.VMEM(cot.shape, bf16),
            pltpu.SemaphoreType.DMA((CHUNKS + 2 + 2 * SIDE + CHUNKS * SIDE,)),
        ],
        name="layer",
    )(*quarter, *others, weight, query, cot, head, low, up, valid, live)


def make_body(mesh):
    segments, parts, heads = (mesh.shape[a] for a in AXES)
    runs = segments // SIDE
    ring = runs * heads

    def shift(v, dx=0, dz=0, opposite=False):
        pairs = []
        for s in range(segments):
            for d in range(parts):
                for m in range(heads):
                    z_lo, x = divmod(s, SIDE)
                    sign = -1 if (opposite and d % CORES) else 1
                    x2 = (x + sign * dx) % SIDE
                    m2, z2 = divmod((m * runs + z_lo + sign * dz) % ring, runs)
                    pairs.append(((s * parts + d) * heads + m, ((z2 * SIDE + x2) * parts + d) * heads + m2))
        return lax.ppermute(v, AXES, pairs)

    def sum_over_mp(v, out):
        far = shift(v, dz=2 * runs, opposite=True)
        near = shift(v, dz=runs)
        prior = shift(v, dz=-runs)
        return ((v.astype(f32) + far.astype(f32)) + (near.astype(f32) + prior.astype(f32))).astype(out)

    def body(
        encoder_image_states,
        frozen_key_value,
        adapter_down_weight,
        adapter_up_weight,
        queries,
        cotangent,
        text_token_length,
        image_tile_count,
    ):
        own = encoder_image_states[0]
        tokens, _ = own.shape
        parallel_index = lax.axis_index("mp")
        segment_index = lax.axis_index("segment")
        lowrank, columns = adapter_up_weight.shape[2:]
        up_key, up_value = adapter_up_weight[0, 0], adapter_up_weight[0, 1]
        down = adapter_down_weight[0]
        fourth = down.shape[0]

        line = jnp.concatenate([own, shift(own, dz=-1), shift(own, dz=2, opposite=True), shift(own, dz=1)], axis=0)

        def quarter_of(k):
            return lax.dynamic_slice_in_dim(line, (parallel_index + k) % heads * fourth, fourth, 1)

        def over_line(v):
            return [v, shift(v, dx=-1), shift(v, dx=2, opposite=True), shift(v, dx=1)]

        quarter = over_line(quarter_of(0))
        image_fourth = jnp.concatenate(quarter, axis=0)
        image_others = over_line(jnp.concatenate([quarter_of(k) for k in range(1, heads)], axis=1))
        rows = image_fourth.shape[0]
        offset = jnp.arange(rows, dtype=jnp.int32)
        x_off, z_off, tok = offset // (runs * tokens), (offset // tokens) % runs, offset % tokens
        position = (
            ((segment_index // SIDE + z_off) % runs) * SIDE + (segment_index % SIDE + x_off) % SIDE
        ) * tokens + tok

        local_weight = frozen_key_value[0].reshape(-1, CORES * columns)
        weight = lax.all_gather(local_weight, "dp", axis=0, tiled=True)
        low = jnp.dot(image_fourth, down, preferred_element_type=f32)
        low = lax.all_gather(low, "mp", axis=0, tiled=True)
        text_rows = queries.shape[2]
        none = jnp.zeros_like(up_key)
        up_both = jnp.concatenate(
            [jnp.concatenate([up_key, none], axis=1), jnp.concatenate([none, up_value], axis=1)], axis=0
        )
        valid = (position < image_tile_count[0] * (rows // TILES)).astype(f32)
        live = (jnp.arange(text_rows, dtype=jnp.int32) < text_token_length[0]).astype(f32)
        valid = jnp.broadcast_to(valid[:, None], (rows, text_rows))
        live = jnp.broadcast_to(live[None, :], (8, text_rows))
        kv_grad, back, low, stay, next_x, far_x, prior_x = layer(
            quarter,
            image_others,
            weight,
            parallel_index.astype(jnp.int32)[None],
            low,
            up_both,
            queries[0, 0],
            cotangent[0, 0],
            valid,
            live,
        )

        image_grad = (
            stay
            + shift(next_x, dx=1).astype(f32)
            + shift(far_x, dx=2, opposite=True).astype(f32)
            + shift(prior_x, dx=-1).astype(f32)
        )

        back = lax.all_gather(back, "mp", axis=0)
        back = jnp.sum(back.astype(f32), axis=0).astype(bf16)
        adapter_grad = lax.dot_general(back, down, contracted_columns, preferred_element_type=f32)
        block = stay.shape[0]
        adapter_away = adapter_grad.astype(bf16)
        adapter_grad = (
            adapter_grad[:block]
            + shift(adapter_away[block : 2 * block], dx=1).astype(f32)
            + shift(adapter_away[2 * block : 3 * block], dx=2, opposite=True).astype(f32)
            + shift(adapter_away[3 * block :], dx=-1).astype(f32)
        )
        here = lax.dynamic_slice_in_dim(image_grad, parallel_index * fourth, fourth, 1)
        image_grad = lax.dynamic_update_slice_in_dim(image_grad, here + adapter_grad, parallel_index * fourth, 1)

        down_grad = lax.dot_general(image_fourth, back, contract_rows, preferred_element_type=f32)
        up_grad = adapter_scale * jnp.stack(
            [
                lax.dot_general(low[:, :lowrank], kv_grad[:, :columns], contract_rows, preferred_element_type=f32),
                lax.dot_general(low[:, lowrank:], kv_grad[:, columns:], contract_rows, preferred_element_type=f32),
            ]
        )
        both = jnp.concatenate([down_grad, up_grad.reshape(-1, down_grad.shape[1])], axis=0)
        both = lax.psum_scatter(both, "dp", scatter_dimension=0, tiled=True)
        both = both.astype(bf16)

        send = image_grad[tokens:].astype(bf16)
        image_grad = (
            image_grad[:tokens]
            + shift(send[:tokens], dz=1).astype(f32)
            + shift(send[tokens : 2 * tokens], dz=2, opposite=True).astype(f32)
            + shift(send[2 * tokens :], dz=-1).astype(f32)
        )
        result = sum_over_mp(image_grad.astype(bf16), f32)
        both = lax.all_gather(both, "dp", axis=0, tiled=True)
        down_out = both[:fourth]
        up_out = both[fourth:].reshape(up_grad.shape)
        return (down_out[None], up_out[None], result[None])

    return body


def solution(mesh):
    in_specs = (
        P("dp", "segment", None),
        P("segment", "dp", None, "mp"),
        P("segment", "mp", None),
        P("segment", None, None, "mp"),
        P("segment", "dp", None, "mp"),
        P("segment", "dp", None, "mp"),
        P("dp"),
        P("dp"),
    )
    out_specs = (P("segment", "mp", None), P("segment", None, None, "mp"), P("dp", "segment", None))
    body = make_body(mesh)

    return jax.shard_map(body, mesh=mesh, in_specs=in_specs, out_specs=out_specs, check_vma=False)
```

```python
import jax
import jax.numpy as jnp
from jax import lax
from jax.experimental import pallas as pl
from jax.experimental.pallas import tpu as pltpu
from jax.sharding import PartitionSpec as P


HD = 128
TILES = 4
SIDE = 4
CORES = 2

adapter_scale = 2.0
contract_rows = (((0,), (0,)), ((), ()))
contracted_columns = (((1,), (1,)), ((), ()))
f32 = jnp.float32
bf16 = jnp.bfloat16
AXES = ("segment", "dp", "mp")


CHUNKS = 8


def layer_kernel(*refs):
    pieces, refs = refs[: 2 * SIDE], refs[2 * SIDE :]
    weight_hbm, query_hbm, cot_hbm, head_ref, low_ref, up_ref, valid_ref, live_ref, *refs = refs
    kv_grad_ref, back_ref, low_out_ref, *rest = refs
    block_hbm, rest = rest[:SIDE], rest[SIDE:]
    own_ref, *away_refs, quarter_ref, others_ref, weight_ref, query_ref, cot_ref, sems = rest
    columns = weight_ref.shape[1] // 2
    local_kv = columns // HD
    group = query_ref.shape[1] // HD // local_kv
    block = own_ref.shape[0]
    share = weight_ref.shape[0] // CHUNKS

    first = quarter_ref.shape[1] // share

    def chunk(c):
        return pl.ds(c * share, share)

    def turned(c):
        return pl.ds(pl.multiple_of((head_ref[0] * first + c) % CHUNKS * share, share), share)

    query_copy = pltpu.make_async_copy(query_hbm, query_ref, sems.at[CHUNKS])
    cot_copy = pltpu.make_async_copy(cot_hbm, cot_ref, sems.at[CHUNKS + 1])
    image_copies = []
    for i, piece in enumerate(pieces):
        target = (quarter_ref if i < SIDE else others_ref).at[pl.ds(i % SIDE * block, block)]
        image_copies.append(pltpu.make_async_copy(piece, target, sems.at[CHUNKS + 2 + i]))
    weight_copies = [
        pltpu.make_async_copy(weight_hbm.at[turned(c)], weight_ref.at[turned(c)], sems.at[c]) for c in range(CHUNKS)
    ]
    for copy in image_copies:
        copy.start()
    for copy in weight_copies:
        copy.start()
    query_copy.start()
    cot_copy.start()

    rows = low_out_ref.shape[0]
    low = sum(low_ref[pl.ds(i * rows, rows), :] for i in range(low_ref.shape[0] // rows)).astype(bf16)
    low_out_ref[...] = low
    key_value = adapter_scale * jnp.dot(low, up_ref[...], preferred_element_type=f32)
    for copy in image_copies:
        copy.wait()
    for c, copy in enumerate(weight_copies):
        copy.wait()
        image = quarter_ref[:, chunk(c)] if c < first else others_ref[:, chunk(c - first)]
        key_value += jnp.dot(image, weight_ref[turned(c), :], preferred_element_type=f32)
    key_value = key_value.astype(bf16)
    query_copy.wait()
    cot_copy.wait()
    valid = valid_ref[...] > 0
    live = live_ref[0:1, :]
    for g in range(local_kv):
        key_at, value_at = g * HD, columns + g * HD
        keys = key_value[:, key_at : key_at + HD]
        values = key_value[:, value_at : value_at + HD]
        key_grad = value_grad = None
        for r in range(group):
            at = (g * group + r) * HD
            query, cot = query_ref[:, at : at + HD], cot_ref[:, at : at + HD]
            scores = lax.dot_general(keys, query, contracted_columns, preferred_element_type=f32) * HD ** (-0.5)
            masked = jnp.where(valid, scores, -1e30)
            shifted = jnp.exp(masked - jnp.max(masked, axis=0, keepdims=True))
            attention = shifted * (1.0 / jnp.sum(shifted, axis=0, keepdims=True))
            dweights = lax.dot_general(values, cot, contracted_columns, preferred_element_type=f32)
            delta = jnp.sum(attention * dweights, axis=0, keepdims=True)
            dscore = (attention * (dweights - delta) * (live * HD ** (-0.5))).astype(bf16)
            kept = (attention * live).astype(bf16)
            dk = jnp.dot(dscore, query, preferred_element_type=f32)
            dv = jnp.dot(kept, cot, preferred_element_type=f32)
            key_grad = dk if r == 0 else key_grad + dk
            value_grad = dv if r == 0 else value_grad + dv
        kv_grad_ref[:, key_at : key_at + HD] = key_grad.astype(bf16)
        kv_grad_ref[:, value_at : value_at + HD] = value_grad.astype(bf16)
    kv_grad = kv_grad_ref[...]
    back = adapter_scale * lax.dot_general(kv_grad, up_ref[...], contracted_columns, preferred_element_type=f32)
    back_ref[...] = back.astype(bf16)
    out_copies = []
    for c in range(CHUNKS):
        total = lax.dot_general(kv_grad, weight_ref[chunk(c), :], contracted_columns, preferred_element_type=f32)
        own_ref[:, chunk(c)] = total[:block].astype(bf16)
        for i, ref in enumerate(away_refs):
            ref[:, chunk(c)] = total[(i + 1) * block : (i + 2) * block].astype(bf16)
        for i, (ref, target) in enumerate(zip((own_ref, *away_refs), block_hbm)):
            copy = pltpu.make_async_copy(
                ref.at[:, chunk(c)], target.at[:, chunk(c)], sems.at[CHUNKS + 2 + 2 * SIDE + c * SIDE + i]
            )
            copy.start()
            out_copies.append(copy)
    for copy in out_copies:
        copy.wait()


def layer(quarter, others, weight, head, low, up, query, cot, valid, live):
    rows, width = SIDE * quarter[0].shape[0], weight.shape[0]
    columns = weight.shape[1]
    rank = low.shape[1]
    block = rows // SIDE
    blocks = [(block, width, bf16)] * SIDE
    outside = pl.BlockSpec(memory_space=pl.ANY)
    inside_vmem = pl.BlockSpec(memory_space=pltpu.VMEM)
    return pl.pallas_call(
        layer_kernel,
        in_specs=[outside] * (2 * SIDE + 3) + [pl.BlockSpec(memory_space=pltpu.SMEM)] + [inside_vmem] * 4,
        out_specs=[inside_vmem] * 3 + [outside] * SIDE,
        out_shape=[
            jax.ShapeDtypeStruct((rows, columns), bf16),
            jax.ShapeDtypeStruct((rows, rank), bf16),
            jax.ShapeDtypeStruct((rows, rank), bf16),
        ]
        + [jax.ShapeDtypeStruct(v[:2], v[2]) for v in blocks],
        scratch_shapes=[pltpu.VMEM(v[:2], v[2]) for v in blocks]
        + [
            pltpu.VMEM((rows, quarter[0].shape[1]), bf16),
            pltpu.VMEM((rows, others[0].shape[1]), bf16),
            pltpu.VMEM(weight.shape, bf16),
            pltpu.VMEM(query.shape, bf16),
            pltpu.VMEM(cot.shape, bf16),
            pltpu.SemaphoreType.DMA((CHUNKS + 2 + 2 * SIDE + CHUNKS * SIDE,)),
        ],
        name="layer",
    )(*quarter, *others, weight, query, cot, head, low, up, valid, live)


def make_body(mesh):
    segments, parts, heads = (mesh.shape[a] for a in AXES)
    runs = segments // SIDE
    ring = runs * heads

    def shift(v, dx=0, dz=0, opposite=False):
        pairs = []
        for s in range(segments):
            for d in range(parts):
                for m in range(heads):
                    z_lo, x = divmod(s, SIDE)
                    sign = -1 if (opposite and d % CORES) else 1
                    x2 = (x + sign * dx) % SIDE
                    m2, z2 = divmod((m * runs + z_lo + sign * dz) % ring, runs)
                    pairs.append(((s * parts + d) * heads + m, ((z2 * SIDE + x2) * parts + d) * heads + m2))
        return lax.ppermute(v, AXES, pairs)

    def sum_over_mp(v, out):
        far = shift(v, dz=2 * runs, opposite=True)
        near = shift(v, dz=runs)
        prior = shift(v, dz=-runs)
        return ((v.astype(f32) + far.astype(f32)) + (near.astype(f32) + prior.astype(f32))).astype(out)

    def body(
        encoder_image_states,
        frozen_key_value,
        adapter_down_weight,
        adapter_up_weight,
        queries,
        cotangent,
        text_token_length,
        image_tile_count,
    ):
        own = encoder_image_states[0]
        tokens, _ = own.shape
        parallel_index = lax.axis_index("mp")
        segment_index = lax.axis_index("segment")
        lowrank, columns = adapter_up_weight.shape[2:]
        up_key, up_value = adapter_up_weight[0, 0], adapter_up_weight[0, 1]
        down = adapter_down_weight[0]
        fourth = down.shape[0]

        line = jnp.concatenate([own, shift(own, dz=-1), shift(own, dz=2, opposite=True), shift(own, dz=1)], axis=0)

        def quarter_of(k):
            return lax.dynamic_slice_in_dim(line, (parallel_index + k) % heads * fourth, fourth, 1)

        def over_line(v):
            return [v, shift(v, dx=-1), shift(v, dx=2, opposite=True), shift(v, dx=1)]

        quarter = over_line(quarter_of(0))
        image_fourth = jnp.concatenate(quarter, axis=0)
        image_others = over_line(jnp.concatenate([quarter_of(k) for k in range(1, heads)], axis=1))
        rows = image_fourth.shape[0]
        offset = jnp.arange(rows, dtype=jnp.int32)
        x_off, z_off, tok = offset // (runs * tokens), (offset // tokens) % runs, offset % tokens
        position = (
            ((segment_index // SIDE + z_off) % runs) * SIDE + (segment_index % SIDE + x_off) % SIDE
        ) * tokens + tok

        local_weight = frozen_key_value[0].reshape(-1, CORES * columns)
        weight = lax.all_gather(local_weight, "dp", axis=0, tiled=True)
        low = jnp.dot(image_fourth, down, preferred_element_type=f32)
        low = lax.all_gather(low, "mp", axis=0, tiled=True)
        text_rows = queries.shape[2]
        none = jnp.zeros_like(up_key)
        up_both = jnp.concatenate(
            [jnp.concatenate([up_key, none], axis=1), jnp.concatenate([none, up_value], axis=1)], axis=0
        )
        valid = (position < image_tile_count[0] * (rows // TILES)).astype(f32)
        live = (jnp.arange(text_rows, dtype=jnp.int32) < text_token_length[0]).astype(f32)
        valid = jnp.broadcast_to(valid[:, None], (rows, text_rows))
        live = jnp.broadcast_to(live[None, :], (8, text_rows))
        kv_grad, back, low, stay, next_x, far_x, prior_x = layer(
            quarter,
            image_others,
            weight,
            parallel_index.astype(jnp.int32)[None],
            low,
            up_both,
            queries[0, 0],
            cotangent[0, 0],
            valid,
            live,
        )

        image_grad = (
            stay.astype(f32)
            + shift(next_x, dx=1).astype(f32)
            + shift(far_x, dx=2, opposite=True).astype(f32)
            + shift(prior_x, dx=-1).astype(f32)
        )

        back = lax.all_gather(back, "mp", axis=0)
        back = jnp.sum(back.astype(f32), axis=0).astype(bf16)
        adapter_grad = lax.dot_general(back, down, contracted_columns, preferred_element_type=f32)
        block = stay.shape[0]
        adapter_away = adapter_grad.astype(bf16)
        adapter_grad = (
            adapter_grad[:block]
            + shift(adapter_away[block : 2 * block], dx=1).astype(f32)
            + shift(adapter_away[2 * block : 3 * block], dx=2, opposite=True).astype(f32)
            + shift(adapter_away[3 * block :], dx=-1).astype(f32)
        )
        here = lax.dynamic_slice_in_dim(image_grad, parallel_index * fourth, fourth, 1)
        image_grad = lax.dynamic_update_slice_in_dim(image_grad, here + adapter_grad, parallel_index * fourth, 1)

        down_grad = lax.dot_general(image_fourth, back, contract_rows, preferred_element_type=f32)
        up_grad = adapter_scale * jnp.stack(
            [
                lax.dot_general(low[:, :lowrank], kv_grad[:, :columns], contract_rows, preferred_element_type=f32),
                lax.dot_general(low[:, lowrank:], kv_grad[:, columns:], contract_rows, preferred_element_type=f32),
            ]
        )
        both = jnp.concatenate([down_grad, up_grad.reshape(-1, down_grad.shape[1])], axis=0)
        both = lax.psum_scatter(both, "dp", scatter_dimension=0, tiled=True)
        both = both.astype(bf16)

        send = image_grad[tokens:].astype(bf16)
        image_grad = (
            image_grad[:tokens]
            + shift(send[:tokens], dz=1).astype(f32)
            + shift(send[tokens : 2 * tokens], dz=2, opposite=True).astype(f32)
            + shift(send[2 * tokens :], dz=-1).astype(f32)
        )
        result = sum_over_mp(image_grad.astype(bf16), f32)
        both = lax.all_gather(both, "dp", axis=0, tiled=True)
        down_out = both[:fourth]
        up_out = both[fourth:].reshape(up_grad.shape)
        return (down_out[None], up_out[None], result[None])

    return body


def solution(mesh):
    in_specs = (
        P("dp", "segment", None),
        P("segment", "dp", None, "mp"),
        P("segment", "mp", None),
        P("segment", None, None, "mp"),
        P("segment", "dp", None, "mp"),
        P("segment", "dp", None, "mp"),
        P("dp"),
        P("dp"),
    )
    out_specs = (P("segment", "mp", None), P("segment", None, None, "mp"), P("dp", "segment", None))
    body = make_body(mesh)

    return jax.shard_map(body, mesh=mesh, in_specs=in_specs, out_specs=out_specs, check_vma=False)
```
